32 devices in a mesh: clip: 2 (over core), row: 4 (over y, x), col: 4 (over z).
Axes of the slice: x: 2, y: 2, z: 4, core: 2. Of those that a mesh axis runs over, the one named last changes fastest.
Arguments:
- video: bfloat16 [2, 8, 64, 64, 128], P('clip', None, 'row', 'col'), may hold values from -6 to 6
- frame_counts: int32 [2], P('clip'), may hold values from 2 to 8, as said below
- kernel_main: bfloat16 [3, 3, 3, 128, 128], replicated, may hold values from -0.109375 to 0.109375
- kernel_down: bfloat16 [3, 3, 128, 128], replicated, may hold values from -0.1875 to 0.1875
- latent_grad: bfloat16 [2, 8, 32, 32, 128], P('clip', None, 'row', 'col'), may hold values from -6 to 6
Outputs:
- latent: bfloat16 [2, 8, 32, 32, 128], P('clip', None, 'row', 'col')
- video_grad: bfloat16 [2, 8, 64, 64, 128], P('clip', None, 'row', 'col')
- main_grad: float32 [3, 3, 3, 128, 128], replicated
- down_grad: float32 [3, 3, 128, 128], replicated
The draws below stay inside these ranges and needn't reach their ends.
Inputs may be any that keep to these rules, and one draw needn't show every extreme that they name: `frame_counts`: some clip has all 8 frames in every draw.
All inputs are finite; a program needn't handle non-finite values.
Results may differ from the reference program's by a relative error of at most 0.005.
Values may be sent and summed in bfloat16 or wider, within the bound.
No kernel may reach another device: no remote copies, remote signals or barrier semaphores. Data moves between devices by JAX's collectives and lax.ppermute only.
A program may use at most 64 MiB of HBM per device.

```python
import jax
import jax.numpy as jnp
from jax import lax

C = 128
F = 8
CLIPS = 2
H = 64
W = 64


def draw_frame_counts(key, part):
    first_key = jax.random.fold_in(key, 11)
    second_key = jax.random.fold_in(key, 23)
    lowest = max(1, F // 4)
    counts = jax.random.randint(first_key, (CLIPS,), lowest, F)
    fullest = jax.random.randint(second_key, (), 0, CLIPS)
    return jnp.where(jnp.arange(CLIPS) == fullest, F, counts).astype(jnp.int32)


def level_of(stream_key, shape, split, smallest, largest):
    def one(dim, parts):
        heights = jax.random.uniform(jax.random.fold_in(jax.random.fold_in(stream_key, 6), dim), (parts,), jnp.float32, smallest / len(split), largest / len(split))
        return jnp.repeat(jnp.exp(heights), shape[dim] // parts).reshape((-1,) + (1,) * (len(shape) - dim - 1))

    loudness = one(*split[0])
    for cut in split[1:]:
        loudness = loudness * one(*cut)
    return loudness


def bell_draw(rng, dims, width, most, pieces=(), held_as=jnp.bfloat16):
    drawn = jax.random.normal(rng, dims, jnp.float32) * width
    if len(pieces) > 0:
        drawn = level_of(rng, dims, pieces, -0.22, 0.18) * drawn
    return jnp.clip(drawn, min=-most, max=most).astype(held_as)


def setup_inputs(seed: int = 0) -> dict:
    streams_of = jax.random.split(jax.random.key(seed), 6)
    video = bell_draw(streams_of[0], (CLIPS, F, H, W, C), 1.0, 6.0, ((0, 2), (2, 4), (3, 4)))
    frame_counts = draw_frame_counts(jax.random.fold_in(streams_of[5], 71), 0)
    kernel_main = bell_draw(streams_of[2], (3, 3, 3, C, C), (27 * C) ** -0.5, 0.109375)
    kernel_down = bell_draw(streams_of[3], (3, 3, C, C), (9 * C) ** -0.5, 0.1875)
    latent_grad = bell_draw(streams_of[4], (CLIPS, F, H // 2, W // 2, C), 1.0, 6.0, ((0, 2), (2, 4), (3, 4)))
    return dict(video=video, frame_counts=frame_counts, kernel_main=kernel_main, kernel_down=kernel_down, latent_grad=latent_grad)


def conv_main(inputs, kernel):
    first = inputs[:, :1]
    stacked = jnp.concatenate([first, first, inputs], axis=1)
    stacked = jnp.pad(stacked, ((0, 0), (0, 0), (1, 1), (1, 1), (0, 0)))
    return lax.conv_general_dilated(stacked, kernel, (1, 1, 1), 'VALID', dimension_numbers=('NDHWC', 'DHWIO', 'NDHWC'), precision=lax.Precision.HIGHEST)

def conv_down(values, kernel):
    padded = jnp.pad(values, ((0, 0), (0, 1), (0, 1), (0, 0)))
    return lax.conv_general_dilated(padded, kernel, (2, 2), 'VALID', dimension_numbers=('NHWC', 'HWIO', 'NHWC'), precision=lax.Precision.HIGHEST)

def reference(video, frame_counts, kernel_main, kernel_down, latent_grad):
    main_float = kernel_main.astype(jnp.float32)
    down_float = kernel_down.astype(jnp.float32)

    def per_clip(packed):
        frames_in, grad_in, count = packed
        video_float = frames_in.astype(jnp.float32)
        pre = conv_main(video_float[None], main_float)[0]
        live = (jnp.arange(F) < count).astype(jnp.float32)[:, None, None, None]
        act = (jax.nn.silu(pre) * live).astype(jnp.bfloat16)
        act = lax.optimization_barrier(act)
        latent_float, pull_down = jax.vjp(conv_down, act.astype(jnp.float32), down_float)
        act_grad, down_part = pull_down(grad_in.astype(jnp.float32))
        logistic = jax.nn.sigmoid(pre)
        pre_grad = (act_grad * logistic * (1.0 + pre * (1.0 - logistic)) * live).astype(jnp.bfloat16)
        pre_grad = lax.optimization_barrier(pre_grad)

        def main_single(values, kernel):
            return conv_main(values[None], kernel)[0]
        unused, pull_main = jax.vjp(main_single, video_float, main_float)
        video_part, main_part = pull_main(pre_grad.astype(jnp.float32))
        return (latent_float.astype(jnp.bfloat16), video_part.astype(jnp.bfloat16), main_part, down_part)
    latent, video_grad, main_parts, down_parts = lax.map(per_clip, (video, latent_grad, frame_counts))
    return (latent, video_grad, lax.optimization_barrier(jnp.sum(main_parts, axis=0)), lax.optimization_barrier(jnp.sum(down_parts, axis=0)))
```

```python
import jax
import jax.numpy as jnp
from jax import lax
from jax.sharding import PartitionSpec as P

BF = jnp.bfloat16
F32 = jnp.float32


def flip(axis, mask):
    return [(i, i ^ mask) for i in range(lax.axis_size(axis))]


def part(x, index, size):
    return lax.dynamic_slice_in_dim(x, index * size, size, axis=0)


def exchange(low_edge, high_edge, axis):
    count = lax.axis_size(axis)
    up = lax.ppermute(high_edge, axis, [(i, i + 1) for i in range(count - 1)])
    down = lax.ppermute(low_edge, axis, [(i + 1, i) for i in range(count - 1)])
    return up, down


def pack(a, b):
    return jnp.concatenate([a.reshape(-1, a.shape[-1]), b.reshape(-1, b.shape[-1])])


def unpack(buffer, a_shape, b_shape):
    rows = a_shape[0] * a_shape[1] * a_shape[2]
    return buffer[:rows].reshape(a_shape), buffer[rows:].reshape(b_shape)


def with_halo(video, grad):
    for axis, dim in (("row", 1), ("col", 2)):
        size, gsize = video.shape[dim], grad.shape[dim]
        v_low = lax.slice_in_dim(video, 0, 2, axis=dim)
        v_high = lax.slice_in_dim(video, size - 2, size, axis=dim)
        g_low = lax.slice_in_dim(grad, 0, 1, axis=dim)
        g_high = lax.slice_in_dim(grad, gsize - 1, gsize, axis=dim)
        before, after = exchange(pack(v_low, g_low), pack(v_high, g_high), axis)
        v_before, g_before = unpack(before, v_low.shape, g_low.shape)
        v_after, g_after = unpack(after, v_low.shape, g_low.shape)
        video = jnp.concatenate([v_before, video, v_after], axis=dim)
        grad = jnp.concatenate([g_before, grad, g_after], axis=dim)
    return video, grad


def direct_scatter(x, axis):
    count, mine = lax.axis_size(axis), lax.axis_index(axis)
    share = x.shape[0] // count
    total = part(x, mine, share)
    for mask in range(1, count):
        sent = part(x, mine ^ mask, share).astype(BF)
        total = total + lax.ppermute(sent, axis, flip(axis, mask)).astype(F32)
    return total


def direct_gather(y, axis):
    count, mine = lax.axis_size(axis), lax.axis_index(axis)
    share = y.shape[0]
    whole = jnp.zeros((count * share,) + y.shape[1:], y.dtype)
    whole = lax.dynamic_update_slice_in_dim(whole, y, mine * share, 0)
    for mask in range(1, count):
        got = lax.ppermute(y, axis, flip(axis, mask))
        whole = lax.dynamic_update_slice_in_dim(whole, got, (mine ^ mask) * share, 0)
    return whole


def reduce_all(x):
    half, core = x.shape[0] // 2, lax.axis_index("clip")
    swap = flip("clip", 1)
    x = part(x, core, half) + lax.ppermute(part(x, 1 - core, half), "clip", swap)
    y = direct_scatter(direct_scatter(x, "row"), "col").astype(BF)
    y = direct_gather(direct_gather(y, "col"), "row")
    other = lax.ppermute(y, "clip", swap)
    both = jnp.where(core == 0, jnp.stack([y, other]), jnp.stack([other, y]))
    return both.reshape(-1, x.shape[-1]).astype(F32)


def conv_three(inputs, kernel):
    return lax.conv_general_dilated(
        inputs,
        kernel,
        (1, 1, 1),
        "VALID",
        dimension_numbers=("NDHWC", "DHWIO", "NDHWC"),
        preferred_element_type=F32,
    )


def inside(axis, tile):
    place = lax.axis_index(axis) * tile + jnp.arange(-1, tile + 1)
    return ((place >= 0) & (place < lax.axis_size(axis) * tile)).astype(F32)


def on_device(video, frame_counts, kernel_main, kernel_down, latent_grad):
    _, frames, rows, cols, channels = video.shape
    wide, grad_wide = with_halo(video[0], latent_grad[0])
    first = wide[:1]
    stacked = jnp.concatenate([first, first, wide])[None]
    live = (jnp.arange(frames) < frame_counts[0]).astype(F32)[:, None, None, None]
    mask = live * (inside("row", rows)[:, None] * inside("col", cols)[None, :])[None, :, :, None]
    pre = conv_three(stacked, kernel_main)[0]
    logistic = jax.nn.sigmoid(pre)
    act = (pre * logistic * mask).astype(BF)[:, 1:, 1:]
    flipped_down = jnp.transpose(kernel_down[::-1, ::-1], (0, 1, 3, 2))
    act_grad = lax.conv_general_dilated(
        grad_wide,
        flipped_down,
        (1, 1),
        ((1, 0), (1, 0)),
        lhs_dilation=(2, 2),
        dimension_numbers=("NHWC", "HWIO", "NHWC"),
        preferred_element_type=F32,
    )[:, :, :]
    act_grad = act_grad[:, : rows + 2, : cols + 2]
    pre_grad = (act_grad * logistic * (1.0 + pre * (1.0 - logistic)) * mask).astype(BF)
    main_term = lax.conv_general_dilated(
        stacked[:, :, 1:-1, 1:-1],
        pre_grad[None, :, 1:-1, 1:-1],
        (1, 1, 1),
        "VALID",
        dimension_numbers=("CDHWN", "IDHWO", "NDHWC"),
        preferred_element_type=F32,
    )
    main_term = jnp.transpose(main_term, (1, 2, 3, 0, 4))
    down_term = lax.conv_general_dilated(
        act,
        latent_grad[0],
        (1, 1),
        "VALID",
        rhs_dilation=(2, 2),
        dimension_numbers=("CHWN", "IHWO", "NHWC"),
        preferred_element_type=F32,
    )
    down_term = jnp.transpose(down_term, (1, 2, 0, 3))
    summed = reduce_all(pack(main_term, down_term))
    latent = lax.conv_general_dilated(
        act,
        kernel_down,
        (2, 2),
        "VALID",
        dimension_numbers=("NHWC", "HWIO", "NHWC"),
        preferred_element_type=F32,
    ).astype(BF)
    grad_padded = jnp.pad(pre_grad, ((2, 2), (0, 0), (0, 0), (0, 0)))[None]
    flipped_main = jnp.transpose(kernel_main[::-1, ::-1, ::-1], (0, 1, 2, 4, 3))
    back = conv_three(grad_padded, flipped_main)[0]
    head = back[2:3] + back[0:1] + back[1:2]
    video_grad = jnp.concatenate([head, back[3:]]).astype(BF)
    main_rows = 27 * channels
    main_grad = summed[:main_rows].reshape(kernel_main.shape)
    down_grad = summed[main_rows:].reshape(kernel_down.shape)
    return (latent[None], video_grad[None], main_grad, down_grad)


def solution(mesh):
    tiles = P("clip", None, "row", "col", None)
    return jax.shard_map(
        on_device,
        mesh=mesh,
        in_specs=(tiles, P("clip"), P(), P(), tiles),
        out_specs=(tiles, tiles, P(), P()),
        check_vma=False,
    )
```

```python
import jax
import jax.numpy as jnp
from jax import lax
from jax.experimental import pallas as pl
from jax.experimental.pallas import tpu as pltpu
from jax.sharding import PartitionSpec as P

BF = jnp.bfloat16
F32 = jnp.float32


def flip(axis, mask):
    return [(i, i ^ mask) for i in range(lax.axis_size(axis))]


def part(x, index, size):
    return lax.dynamic_slice_in_dim(x, index * size, size, axis=0)


def exchange(low_edge, high_edge, axis):
    count = lax.axis_size(axis)
    up = lax.ppermute(high_edge, axis, [(i, i + 1) for i in range(count - 1)])
    down = lax.ppermute(low_edge, axis, [(i + 1, i) for i in range(count - 1)])
    return up, down


def pack(a, b):
    return jnp.concatenate([a.reshape(-1, a.shape[-1]), b.reshape(-1, b.shape[-1])])


def unpack(buffer, a_shape, b_shape):
    rows = a_shape[0] * a_shape[1] * a_shape[2]
    return buffer[:rows].reshape(a_shape), buffer[rows:].reshape(b_shape)


def with_halo(video, grad):
    for axis, dim in (("row", 1), ("col", 2)):
        size, gsize = video.shape[dim], grad.shape[dim]
        v_low = lax.slice_in_dim(video, 0, 2, axis=dim)
        v_high = lax.slice_in_dim(video, size - 2, size, axis=dim)
        g_low = lax.slice_in_dim(grad, 0, 1, axis=dim)
        g_high = lax.slice_in_dim(grad, gsize - 1, gsize, axis=dim)
        before, after = exchange(pack(v_low, g_low), pack(v_high, g_high), axis)
        v_before, g_before = unpack(before, v_low.shape, g_low.shape)
        v_after, g_after = unpack(after, v_low.shape, g_low.shape)
        video = jnp.concatenate([v_before, video, v_after], axis=dim)
        grad = jnp.concatenate([g_before, grad, g_after], axis=dim)
    return video, grad


def direct_scatter(x, axis, beside):
    count, mine = lax.axis_size(axis), lax.axis_index(axis)
    share = x.shape[0] // count
    got = []
    for mask in range(1, count):
        sent = part(x, mine ^ mask, share).astype(BF)
        got.append(lax.ppermute(sent, axis, flip(axis, mask)))
    got, beside = lax.optimization_barrier((got, beside))
    total = part(x, mine, share)
    for term in got:
        total = total + term.astype(F32)
    return total, beside


def line_sum(x, axis):
    bits, mine = lax.axis_size(axis).bit_length() - 1, lax.axis_index(axis)
    for bit in range(bits - 1):
        side, half = (mine >> bit) & 1, x.shape[0] // 2
        sent = part(x, 1 - side, half).astype(BF)
        x = part(x, side, half) + lax.ppermute(sent, axis, flip(axis, 1 << bit)).astype(F32)
    x = lax.reduce_precision(x, 8, 7)
    got = lax.ppermute(x.astype(BF), axis, flip(axis, 1 << (bits - 1)))
    y = (x + got.astype(F32)).astype(BF)
    for bit in reversed(range(bits - 1)):
        got = lax.ppermute(y, axis, flip(axis, 1 << bit))
        low = ((mine >> bit) & 1) == 0
        y = jnp.where(low, jnp.stack([y, got]), jnp.stack([got, y])).reshape(-1, y.shape[-1])
    return y


def direct_gather(y, axis):
    count, mine = lax.axis_size(axis), lax.axis_index(axis)
    share = y.shape[0]
    whole = jnp.zeros((count * share,) + y.shape[1:], y.dtype)
    whole = lax.dynamic_update_slice_in_dim(whole, y, mine * share, 0)
    for mask in range(1, count):
        got = lax.ppermute(y, axis, flip(axis, mask))
        whole = lax.dynamic_update_slice_in_dim(whole, got, (mine ^ mask) * share, 0)
    return whole


def join_kernel(core, mine, other, main_grad, down_grad):
    split, end = mine.shape[0], main_grad.shape[0]
    for which, low, high in ((0, mine, other), (1, other, mine)):

        @pl.when(core[0] == which)
        def _():
            main_grad[0:split] = low[...].astype(F32)
            main_grad[split:end] = high[0 : end - split].astype(F32)
            down_grad[...] = high[end - split :].astype(F32)


def reduce_all(kept, sent, beside, main_rows):
    half, core = kept.shape[0], lax.axis_index("clip")
    swap = flip("clip", 1)
    x = kept + lax.ppermute(sent, "clip", swap)
    x, beside = direct_scatter(x, "row", beside)
    y = direct_gather(line_sum(x, "col"), "row")
    other = lax.ppermute(y, "clip", swap)
    vmem = pl.BlockSpec(memory_space=pltpu.VMEM)
    main_grad, down_grad = pl.pallas_call(
        join_kernel,
        out_shape=(
            jax.ShapeDtypeStruct((main_rows, x.shape[1]), F32),
            jax.ShapeDtypeStruct((2 * half - main_rows, x.shape[1]), F32),
        ),
        in_specs=[pl.BlockSpec(memory_space=pltpu.SMEM), vmem, vmem],
        out_specs=(vmem, vmem),
        compiler_params=pltpu.CompilerParams(vmem_limit_bytes=8 << 20),
    )(core[None], y, other)
    return main_grad, down_grad, beside


def dot(a, b):
    return lax.dot_general(a, b, (((1,), (0,)), ((), ())), preferred_element_type=F32)


LEFT = 8


def main_kernel(
    flags, wide, grad_wide, kernel_main, w_grad, w_down, latent_grad,
    kept, sent, grad_taps, latent,
    w_main, x32, side32, x_taps, pre, l32, act_grad, act_side, pre_grad, act, act_taps, grad_t,
    total, down_total,
):
    frames, in_rows, in_cols, channels = wide.shape
    rows, cols = in_rows - 4, in_cols - 4
    ext = rows + 2
    half_rows, half_cols = rows // 2, cols // 2
    own, side = ext * cols, ext * 8
    side32[...] = jnp.zeros_like(side32)
    pre[0:2] = jnp.zeros((2,) + pre.shape[1:], F32)
    grad_t[frames:] = jnp.zeros((2,) + grad_t.shape[1:], BF)
    l32[...] = jnp.zeros_like(l32)
    act_side[...] = jnp.zeros_like(act_side)
    for kt in range(3):
        for tap in range(9):
            rows_at, cols_at = tap * channels, kt * channels
            w_main[rows_at : rows_at + channels, cols_at : cols_at + channels] = kernel_main[9 * kt + tap]
    count = flags[0]
    low_row, high_row = flags[1].astype(F32), flags[2].astype(F32)
    low_col, high_col = flags[3].astype(F32), flags[4].astype(F32)

    def frame(t, carry):
        x32[:, 0:in_cols, :] = wide[t].astype(F32)
        for kw in range(3):
            shifted = x32[:, pl.ds(1 + kw, cols), :].astype(BF)
            x_taps[t, kw] = shifted.reshape(in_rows * cols, channels)
            side32[kw, :, 0:1, :] = x32[:, kw : kw + 1, :]
            side32[kw, :, 1:2, :] = x32[:, cols + 1 + kw : cols + 2 + kw, :]
        lhs = jnp.concatenate(
            [
                x_taps[t, kw, kh * cols : kh * cols + own]
                for kh in range(3)
                for kw in range(3)
            ],
            axis=1,
        )
        side_lhs = jnp.concatenate(
            [
                side32[kw, kh : kh + ext].reshape(side, channels).astype(BF)
                for kh in range(3)
                for kw in range(3)
            ],
            axis=1,
        )
        for start, size, left in ((0, own, lhs), (own, side, side_lhs)):
            out = dot(left, w_main[...])
            place = pl.ds(start, size)
            parts = [out[:, k * channels : (k + 1) * channels] for k in range(3)]
            pre[t + 2, place] = parts[0]
            pre[t + 1, place] += parts[1]
            pre[t, place] += parts[2]

            @pl.when(t == 0)
            def _():
                pre[0, place] += parts[0] + parts[1]
                pre[1, place] += parts[0]

        l32[:, 0 : half_cols + 2, :] = grad_wide[t].astype(F32)
        near = [l32[:, pl.ds(dq, 16), :].astype(BF) for dq in range(2)]
        grads = jnp.concatenate(
            [
                near[dq][dp : dp + half_rows + 1].reshape((half_rows + 1) * 16, channels)
                for dp in (1, 0)
                for dq in (1, 0)
            ],
            axis=1,
        )
        classes = dot(grads, w_grad[...])
        for p in range(half_rows + 1):
            for odd in range(2):
                line = classes[p * 16 : p * 16 + half_cols + 1]
                row = 2 * p + 1 - odd
                even_part = line[:, 2 * odd * channels : (2 * odd + 1) * channels]
                odd_part = line[:, (2 * odd + 1) * channels : (2 * odd + 2) * channels]
                act_grad[row, pl.ds(LEFT, half_cols + 1, stride=2), :] = even_part
                act_grad[row, pl.ds(LEFT - 1, half_cols + 1, stride=2), :] = odd_part
        act_side[:, 0:1, :] = act_grad[:, LEFT - 1 : LEFT, :]
        act_side[:, 1:2, :] = act_grad[:, LEFT + cols : LEFT + cols + 1, :]

        live = jnp.where(t < count, 1.0, 0.0).astype(F32)

        def row_mask(width):
            place = lax.broadcasted_iota(jnp.int32, (ext, width, channels), 0)
            edge = jnp.where(place == 0, low_row, jnp.where(place == ext - 1, high_row, 1.0))
            return edge * live

        def pointwise(v, grad, mask):
            logistic = 1.0 / (1.0 + jnp.exp(-v))
            out = (v * logistic * mask).astype(BF)
            back = (grad * logistic * (1.0 + v * (1.0 - logistic)) * mask).astype(BF)
            return out.astype(F32), back

        own_act, own_grad = pointwise(
            pre[t, 0:own],
            act_grad[:, LEFT : LEFT + cols, :].reshape(own, channels),
            row_mask(cols).reshape(own, channels),
        )
        act[:, LEFT : LEFT + cols, :] = own_act.reshape(ext, cols, channels)
        pre_grad[:, LEFT : LEFT + cols, :] = own_grad.astype(F32).reshape(ext, cols, channels)
        inner = own_grad[cols : cols + rows * cols].astype(F32)
        grad_t[t] = inner.T.astype(BF)
        place = lax.broadcasted_iota(jnp.int32, (ext, 8, channels), 1)
        col_mask = jnp.where(place == 0, low_col, jnp.where(place == 1, high_col, 0.0))
        rim_act, rim_grad = pointwise(
            pre[t, own : own + side],
            act_side[...].reshape(side, channels),
            (row_mask(8) * col_mask).reshape(side, channels),
        )
        rim_act = rim_act.reshape(ext, 8, channels)
        rim_grad = rim_grad.astype(F32).reshape(ext, 8, channels)
        act[:, LEFT + cols : LEFT + cols + 1, :] = rim_act[:, 1:2, :]
        pre_grad[:, LEFT - 1 : LEFT, :] = rim_grad[:, 0:1, :]
        pre_grad[:, LEFT + cols : LEFT + cols + 1, :] = rim_grad[:, 1:2, :]
        for kw in range(3):
            shifted = pre_grad[:, pl.ds(LEFT - 1 + kw, cols), :].astype(BF)
            grad_taps[t, kw] = shifted.reshape(own, channels)
        for a in range(3):
            for b in range(3):
                tap = jnp.concatenate(
                    [
                        act[2 * i + a + 1, pl.ds(LEFT + b, half_cols, stride=2), :]
                        for i in range(half_rows)
                    ],
                    axis=0,
                ).astype(BF)
                at = (3 * a + b) * channels
                act_taps[t, :, at : at + channels] = tap
        return carry

    lax.fori_loop(0, frames, frame, 0)

    flat = act_taps[...].reshape(frames * half_rows * half_cols, 9 * channels)
    latent[...] = dot(flat, w_down[...]).astype(BF)
    down = dot(latent_grad[...].astype(F32).T.astype(BF), flat)
    for tap in range(9):
        down_total[tap] = down[:, tap * channels : (tap + 1) * channels]

    total[...] = jnp.zeros_like(total)

    def weights(s, carry):
        right = jnp.concatenate(
            [
                x_taps[s, kw, (kh + 1) * cols : (kh + 1 + rows) * cols]
                for kh in range(3)
                for kw in range(3)
            ],
            axis=1,
        )
        left = grad_t[pl.ds(s, 3)].reshape(3 * channels, rows * cols)
        out = dot(left, right)
        for tap in range(9):
            block = out[:, tap * channels : (tap + 1) * channels]
            total[tap] += block

        @pl.when(s == 0)
        def _():
            for tap in range(9):
                block = out[:, tap * channels : (tap + 1) * channels]
                top, middle = block[:channels], block[channels : 2 * channels]
                total[tap, channels : 2 * channels] += top
                total[tap, 2 * channels :] += top + middle

        return carry

    lax.fori_loop(0, frames, weights, 0)

    def emit(low, high):
        def tap_out(tap, carry):
            at = pl.multiple_of(tap * channels, channels)
            after = pl.multiple_of((9 + tap) * channels, channels)
            low[pl.ds(at, channels), :] = total[tap, 2 * channels :].T
            low[pl.ds(after, channels), :] = total[tap, channels : 2 * channels].T
            high[pl.ds(at, channels), :] = total[tap, 0:channels].T
            high[pl.ds(after, channels), :] = down_total[tap].T
            return carry

        lax.fori_loop(0, 9, tap_out, 0)

    @pl.when(flags[5] == 0)
    def _():
        emit(kept, sent)

    @pl.when(flags[5] == 1)
    def _():
        emit(sent, kept)


def back_kernel(grad_taps, kernel_main, video_grad, w_back, total):
    frames, _, own, channels = grad_taps.shape
    inner = video_grad.shape[1]
    cols = (own - inner) // 2
    total[0:2] = jnp.zeros((2,) + total.shape[1:], F32)
    for kt in range(3):
        for tap in range(9):
            rows_at, cols_at = tap * channels, kt * channels
            block = kernel_main[9 * kt + 8 - tap].astype(F32).T.astype(BF)
            w_back[rows_at : rows_at + channels, cols_at : cols_at + channels] = block

    def frame(t, carry):
        lhs = jnp.concatenate(
            [
                grad_taps[t, kw, kh * cols : kh * cols + inner]
                for kh in range(3)
                for kw in range(3)
            ],
            axis=1,
        )
        out = dot(lhs, w_back[...])
        total[t + 2] = out[:, 2 * channels :]
        total[t + 1] += out[:, channels : 2 * channels]
        total[t] += out[:, :channels]
        return carry

    lax.fori_loop(0, frames, frame, 0)
    video_grad[0] = (total[0] + total[1] + total[2]).astype(BF)

    def store(t, carry):
        video_grad[t] = total[t + 2].astype(BF)
        return carry

    lax.fori_loop(1, frames, store, 0)


def grad_matrix(kernel_down):
    k = jnp.swapaxes(kernel_down, 2, 3)
    zero = jnp.zeros_like(k[0, 0])
    return jnp.concatenate(
        [
            jnp.concatenate([k[0, 0], zero, zero, zero], axis=1),
            jnp.concatenate([k[0, 2], k[0, 1], zero, zero], axis=1),
            jnp.concatenate([k[2, 0], zero, k[1, 0], zero], axis=1),
            jnp.concatenate([k[2, 2], k[2, 1], k[1, 2], k[1, 1]], axis=1),
        ]
    )


def on_device(video, frame_counts, kernel_main, kernel_down, latent_grad):
    _, frames, rows, cols, channels = video.shape
    wide, grad_wide = with_halo(video[0], latent_grad[0])
    row, col = lax.axis_index("row"), lax.axis_index("col")
    flags = jnp.stack(
        [
            frame_counts[0],
            (row > 0).astype(jnp.int32),
            (row < lax.axis_size("row") - 1).astype(jnp.int32),
            (col > 0).astype(jnp.int32),
            (col < lax.axis_size("col") - 1).astype(jnp.int32),
            lax.axis_index("clip"),
        ]
    )
    taps = kernel_main.reshape(27, channels, channels)
    w_down = kernel_down.reshape(9 * channels, channels)
    ext = rows + 2
    own, side, outs = ext * cols, ext * 8, frames * rows * cols // 4
    pixels = frames * rows * cols
    vmem = pl.BlockSpec(memory_space=pltpu.VMEM)
    kept, sent, grad_taps, latent = pl.pallas_call(
        main_kernel,
        out_shape=(
            jax.ShapeDtypeStruct((18 * channels, channels), F32),
            jax.ShapeDtypeStruct((18 * channels, channels), F32),
            jax.ShapeDtypeStruct((frames, 3, own, channels), BF),
            jax.ShapeDtypeStruct((outs, channels), BF),
        ),
        in_specs=[pl.BlockSpec(memory_space=pltpu.SMEM)] + [vmem] * 6,
        out_specs=(vmem,) * 4,
        scratch_shapes=[
            pltpu.VMEM((9 * channels, 3 * channels), BF),
            pltpu.VMEM((rows + 4, cols + 8, channels), F32),
            pltpu.VMEM((3, rows + 4, 8, channels), F32),
            pltpu.VMEM((frames, 3, (rows + 4) * cols, channels), BF),
            pltpu.VMEM((frames + 2, own + side, channels), F32),
            pltpu.VMEM((rows // 2 + 2, 24, channels), F32),
            pltpu.VMEM((ext, cols + 16, channels), F32),
            pltpu.VMEM((ext, 8, channels), F32),
            pltpu.VMEM((ext, cols + 16, channels), F32),
            pltpu.VMEM((ext, cols + 16, channels), F32),
            pltpu.VMEM((frames, rows * cols // 4, 9 * channels), BF),
            pltpu.VMEM((frames + 2, channels, rows * cols), BF),
            pltpu.VMEM((9, 3 * channels, channels), F32),
            pltpu.VMEM((9, channels, channels), F32),
        ],
        compiler_params=pltpu.CompilerParams(vmem_limit_bytes=24 << 20),
        cost_estimate=pl.CostEstimate(
            flops=2 * 60 * pixels * channels * channels,
            bytes_accessed=12 << 20,
            transcendentals=pixels * channels,
        ),
    )(
        flags,
        wide,
        grad_wide,
        taps,
        grad_matrix(kernel_down),
        w_down,
        latent_grad.reshape(outs, channels),
    )
    video_grad = pl.pallas_call(
        back_kernel,
        out_shape=jax.ShapeDtypeStruct((frames, rows * cols, channels), BF),
        in_specs=[vmem] * 2,
        out_specs=vmem,
        scratch_shapes=[
            pltpu.VMEM((9 * channels, 3 * channels), BF),
            pltpu.VMEM((frames + 2, rows * cols, channels), F32),
        ],
        compiler_params=pltpu.CompilerParams(vmem_limit_bytes=12 << 20),
        cost_estimate=pl.CostEstimate(
            flops=2 * 27 * pixels * channels * channels,
            bytes_accessed=4 << 20,
            transcendentals=0,
        ),
    )(grad_taps, taps)
    main_grad, down_grad, video_grad = reduce_all(kept, sent, video_grad, 27 * channels)
    main_grad = main_grad.reshape(kernel_main.shape)
    down_grad = down_grad.reshape(kernel_down.shape)
    return (latent.reshape(latent_grad.shape), video_grad.reshape(video.shape), main_grad, down_grad)


def solution(mesh):
    tiles = P("clip", None, "row", "col", None)
    return jax.shard_map(
        on_device,
        mesh=mesh,
        in_specs=(tiles, P("clip"), P(), P(), tiles),
        out_specs=(tiles, tiles, P(), P()),
        check_vma=False,
    )
```

```python
import jax
import jax.numpy as jnp
from jax import lax
from jax.experimental import pallas as pl
from jax.experimental.pallas import tpu as pltpu
from jax.sharding import PartitionSpec as P

BF = jnp.bfloat16
F32 = jnp.float32


def flip(axis, mask):
    return [(i, i ^ mask) for i in range(lax.axis_size(axis))]


def part(x, index, size):
    return lax.dynamic_slice_in_dim(x, index * size, size, axis=0)


def exchange(low_edge, high_edge, axis):
    count = lax.axis_size(axis)
    even = lax.axis_index(axis) % 2 == 0
    inner = [(i, i ^ 1) for i in range(count - count % 2)]
    outer = [(i, ((i + 1) ^ 1) - 1) for i in range(1, count - 1 + count % 2)]
    a = lax.ppermute(jnp.where(even, high_edge, low_edge), axis, inner)
    b = lax.ppermute(jnp.where(even, low_edge, high_edge), axis, outer)
    return jnp.where(even, b, a), jnp.where(even, a, b)


def pack(a, b):
    return jnp.concatenate([a.reshape(-1, a.shape[-1]), b.reshape(-1, b.shape[-1])])


def unpack(buffer, a_shape, b_shape):
    rows = a_shape[0] * a_shape[1] * a_shape[2]
    return buffer[:rows].reshape(a_shape), buffer[rows:].reshape(b_shape)


def edges(video, grad, dim):
    size, gsize = video.shape[dim], grad.shape[dim]
    cut = lax.slice_in_dim
    low = cut(video, 0, 2, axis=dim), cut(grad, 0, 1, axis=dim)
    high = cut(video, size - 2, size, axis=dim), cut(grad, gsize - 1, gsize, axis=dim)
    return low, high


def joined(video, grad, low, high, before, after, dim):
    v_before, g_before = unpack(before, low[0].shape, low[1].shape)
    v_after, g_after = unpack(after, low[0].shape, low[1].shape)
    video = jnp.concatenate([v_before, video, v_after], axis=dim)
    return video, jnp.concatenate([g_before, grad, g_after], axis=dim)


def with_halo(video, grad, forward):
    low, high = edges(video, grad, 1)
    before, after = exchange(pack(*low), pack(*high), "row")
    tall, grad = joined(video, grad, low, high, before, after, 1)
    low, high = edges(tall, grad, 2)
    before, after = exchange(pack(*low), pack(*high), "col")
    (before, after), ready = lax.optimization_barrier(((before, after), forward(tall)))
    return joined(tall, grad, low, high, before, after, 2) + (ready,)


def direct_scatter(x, axis, beside):
    count, mine = lax.axis_size(axis), lax.axis_index(axis)
    share = x.shape[0] // count
    got = []
    for mask in range(1, count):
        sent = part(x, mine ^ mask, share).astype(BF)
        got.append(lax.ppermute(sent, axis, flip(axis, mask)))
    got, beside = lax.optimization_barrier((got, beside))
    total = part(x, mine, share)
    for term in got:
        total = total + term.astype(F32)
    return total, beside


def line_sum(x, axis):
    bits, mine = lax.axis_size(axis).bit_length() - 1, lax.axis_index(axis)
    for bit in range(bits - 1):
        side, half = (mine >> bit) & 1, x.shape[0] // 2
        sent = part(x, 1 - side, half).astype(BF)
        x = part(x, side, half) + lax.ppermute(sent, axis, flip(axis, 1 << bit)).astype(F32)
    x = lax.reduce_precision(x, 8, 7)
    got = lax.ppermute(x.astype(BF), axis, flip(axis, 1 << (bits - 1)))
    y = (x + got.astype(F32)).astype(BF)
    for bit in reversed(range(bits - 1)):
        got = lax.ppermute(y, axis, flip(axis, 1 << bit))
        low = ((mine >> bit) & 1) == 0
        y = jnp.where(low, jnp.stack([y, got]), jnp.stack([got, y])).reshape(-1, y.shape[-1])
    return y


def direct_gather(y, axis):
    count, mine = lax.axis_size(axis), lax.axis_index(axis)
    share = y.shape[0]
    whole = jnp.zeros((count * share,) + y.shape[1:], y.dtype)
    whole = lax.dynamic_update_slice_in_dim(whole, y, mine * share, 0)
    for mask in range(1, count):
        got = lax.ppermute(y, axis, flip(axis, mask))
        whole = lax.dynamic_update_slice_in_dim(whole, got, (mine ^ mask) * share, 0)
    return whole


def join_kernel(core, mine, other, main_grad, down_grad):
    split, end = mine.shape[0], main_grad.shape[0]
    for which, low, high in ((0, mine, other), (1, other, mine)):

        @pl.when(core[0] == which)
        def _():
            main_grad[0:split] = low[...].astype(F32)
            main_grad[split:end] = high[0 : end - split].astype(F32)
            down_grad[...] = high[end - split :].astype(F32)


def reduce_all(kept, sent, beside, main_rows):
    half, core = kept.shape[0], lax.axis_index("clip")
    swap = flip("clip", 1)
    x = kept + lax.ppermute(sent, "clip", swap).astype(F32)
    x, beside = direct_scatter(x, "row", beside)
    y = direct_gather(line_sum(x, "col"), "row")
    other = lax.ppermute(y, "clip", swap)
    vmem = pl.BlockSpec(memory_space=pltpu.VMEM)
    main_grad, down_grad = pl.pallas_call(
        join_kernel,
        out_shape=(
            jax.ShapeDtypeStruct((main_rows, x.shape[1]), F32),
            jax.ShapeDtypeStruct((2 * half - main_rows, x.shape[1]), F32),
        ),
        in_specs=[pl.BlockSpec(memory_space=pltpu.SMEM), vmem, vmem],
        out_specs=(vmem, vmem),
        compiler_params=pltpu.CompilerParams(vmem_limit_bytes=8 << 20),
    )(core[None], y, other)
    return main_grad, down_grad, beside


def dot(a, b):
    return lax.dot_general(a, b, (((1,), (0,)), ((), ())), preferred_element_type=F32)


LEFT = 8


GROUP = 4
PAIR = 8


def forward_kernel(tall, kernel_main, pre, w_main, x32, x_taps):
    frames, in_rows, cols, channels = tall.shape
    own = (in_rows - 2) * cols
    for kt in range(3):
        for tap in range(9):
            rows_at, cols_at = tap * channels, kt * channels
            w_main[rows_at : rows_at + channels, cols_at : cols_at + channels] = kernel_main[9 * kt + tap]
    pre[0:2] = jnp.zeros((2,) + pre.shape[1:], F32)
    x32[...] = jnp.zeros_like(x32)

    def group(i, carry):
        lines = []
        for g in range(GROUP):
            t = i * GROUP + g
            x32[:, LEFT : LEFT + cols, :] = tall[t].astype(F32)
            for kw in range(3):
                shifted = x32[:, pl.ds(LEFT - 1 + kw, cols), :].astype(BF)
                x_taps[g, kw] = shifted.reshape(in_rows * cols, channels)
            taps = [x_taps[g, kw, kh * cols : kh * cols + own] for kh in range(3) for kw in range(3)]
            lines.append(jnp.concatenate(taps, axis=1))
        out = dot(jnp.concatenate(lines, axis=0), w_main[...])
        parts = [out[:, k * channels : (k + 1) * channels] for k in range(3)]
        for g in range(GROUP):
            t, here = i * GROUP + g, slice(g * own, (g + 1) * own)
            pre[t + 2] = parts[0][here]
            pre[t + 1] += parts[1][here]
            pre[t] += parts[2][here]

        @pl.when(i == 0)
        def _():
            pre[0] += parts[0][:own] + parts[1][:own]
            pre[1] += parts[0][:own]

        return carry

    lax.fori_loop(0, frames // GROUP, group, 0)


def causal(out, channels):
    first, second, third = (out[..., k * channels : (k + 1) * channels] for k in range(3))
    frames = out.shape[-2]
    start = first[..., 0:1, :]
    back_two = jnp.concatenate([start, start, first[..., : frames - 2, :]], axis=-2)
    back_one = jnp.concatenate([second[..., 0:1, :], second[..., : frames - 1, :]], axis=-2)
    return third + back_one + back_two


def pointwise(v, grad, mask):
    logistic = 1.0 / (1.0 + jnp.exp(-v))
    out = (v * logistic * mask).astype(BF)
    back = (grad * logistic * (1.0 + v * (1.0 - logistic)) * mask).astype(BF)
    return out.astype(F32), back.astype(F32)


def main_kernel(
    flags, wide, grad_wide, pre, w_main, w_grad, w_down, latent_grad,
    kept, sent, grad_taps, latent,
    x32, side32, x_taps, v32, fix, l32, act_grad, side_back, side_act, side_grad, pre_grad, act,
    act_taps, grad_t, total, down_total,
):
    frames, in_rows, in_cols, channels = wide.shape
    rows, cols = in_rows - 4, in_cols - 4
    ext = rows + 2
    half_rows, half_cols = rows // 2, cols // 2
    own = ext * cols
    grad_t[frames:] = jnp.zeros((2,) + grad_t.shape[1:], BF)
    l32[...] = jnp.zeros_like(l32)
    count = flags[0]
    low_row, high_row = flags[1].astype(F32), flags[2].astype(F32)
    low_col, high_col = flags[3].astype(F32), flags[4].astype(F32)

    def spread(t, carry):
        x32[:, 0:in_cols, :] = wide[t].astype(F32)
        for kw in range(3):
            shifted = x32[:, pl.ds(1 + kw, cols), :].astype(BF)
            x_taps[t, kw] = shifted.reshape(in_rows * cols, channels)
            side32[kw, :, pl.ds(t, 1), :] = x32[:, kw : kw + 1, :]
            side32[kw, :, pl.ds(frames + t, 1), :] = x32[:, cols + 1 + kw : cols + 2 + kw, :]
        l32[:, 0 : half_cols + 2, :] = grad_wide[t].astype(F32)
        near = [l32[:, pl.ds(dq, 16), :].astype(BF) for dq in range(2)]
        grads = jnp.concatenate(
            [
                near[dq][dp : dp + half_rows + 1].reshape((half_rows + 1) * 16, channels)
                for dp in (1, 0)
                for dq in (1, 0)
            ],
            axis=1,
        )
        classes = dot(grads, w_grad[...])
        for p in range(half_rows + 1):
            for odd in range(2):
                line = classes[p * 16 : p * 16 + half_cols + 1]
                row = 2 * p + 1 - odd
                even_part = line[:, 2 * odd * channels : (2 * odd + 1) * channels]
                odd_part = line[:, (2 * odd + 1) * channels : (2 * odd + 2) * channels]
                act_grad[t, row, pl.ds(LEFT, half_cols + 1, stride=2), :] = even_part
                act_grad[t, row, pl.ds(LEFT - 1, half_cols + 1, stride=2), :] = odd_part
        side_back[:, pl.ds(t, 1), :] = act_grad[t, :, LEFT - 1 : LEFT, :]
        side_back[:, pl.ds(frames + t, 1), :] = act_grad[t, :, LEFT + cols : LEFT + cols + 1, :]
        return carry

    lax.fori_loop(0, frames, spread, 0)

    side_lhs = jnp.concatenate(
        [
            side32[kw, kh : kh + ext].reshape(ext * 2 * frames, channels).astype(BF)
            for kh in range(3)
            for kw in range(3)
        ],
        axis=1,
    )
    side_pre = dot(side_lhs, w_main[...]).reshape(ext, 2, frames, 3 * channels)
    side_pre = causal(side_pre, channels).reshape(ext, 2 * frames, channels)
    for side in range(2):
        at = side * frames
        lhs = jnp.concatenate(
            [
                side32[1, kh : kh + ext, at : at + frames].reshape(ext * frames, channels).astype(BF)
                for kh in range(3)
            ],
            axis=1,
        )
        weights_here = jnp.concatenate(
            [
                w_main[(3 * kh + 2 * side) * channels : (3 * kh + 2 * side + 1) * channels]
                for kh in range(3)
            ],
            axis=0,
        )
        out = dot(lhs, weights_here).reshape(ext, frames, 3 * channels)
        fix[:, at : at + frames, :] = causal(out, channels)

    def row_mask(width):
        place = lax.broadcasted_iota(jnp.int32, (ext, width, channels), 0)
        return jnp.where(place == 0, low_row, jnp.where(place == ext - 1, high_row, 1.0))

    place = lax.broadcasted_iota(jnp.int32, (ext, 2 * frames, channels), 1)
    side_mask = jnp.where(place < frames, low_col, high_col)
    side_mask = jnp.where(place % frames < count, side_mask, 0.0) * row_mask(2 * frames)
    side_act[...], side_grad[...] = pointwise(side_pre, side_back[...], side_mask)

    def frame(t, carry):
        live = jnp.where(t < count, 1.0, 0.0).astype(F32)
        last = frames + t
        v32[...] = pre[t].reshape(ext, cols, channels)
        v32[:, 0:1, :] += fix[:, pl.ds(t, 1), :]
        v32[:, cols - 1 : cols, :] += fix[:, pl.ds(last, 1), :]
        own_act, own_grad = pointwise(
            v32[...], act_grad[t, :, LEFT : LEFT + cols, :], row_mask(cols) * live
        )
        act[:, LEFT : LEFT + cols, :] = own_act
        act[:, LEFT + cols : LEFT + cols + 1, :] = side_act[:, pl.ds(last, 1), :]
        pre_grad[:, LEFT : LEFT + cols, :] = own_grad
        pre_grad[:, LEFT - 1 : LEFT, :] = side_grad[:, pl.ds(t, 1), :]
        pre_grad[:, LEFT + cols : LEFT + cols + 1, :] = side_grad[:, pl.ds(last, 1), :]
        inner = own_grad.reshape(own, channels)[cols : cols + rows * cols]
        grad_t[t] = inner.T.astype(BF)
        for kw in range(3):
            shifted = pre_grad[:, pl.ds(LEFT - 1 + kw, cols), :].astype(BF)
            grad_taps[t, kw] = shifted.reshape(own, channels)
        for a in range(3):
            for b in range(3):
                tap = jnp.concatenate(
                    [
                        act[2 * i + a + 1, pl.ds(LEFT + b, half_cols, stride=2), :]
                        for i in range(half_rows)
                    ],
                    axis=0,
                ).astype(BF)
                at = (3 * a + b) * channels
                act_taps[t, :, at : at + channels] = tap
        return carry

    lax.fori_loop(0, frames, frame, 0)

    flat = act_taps[...].reshape(frames * half_rows * half_cols, 9 * channels)
    latent[...] = dot(flat, w_down[...]).astype(BF)
    down = dot(latent_grad[...].astype(F32).T.astype(BF), flat)
    for tap in range(9):
        down_total[tap] = down[:, tap * channels : (tap + 1) * channels]

    def patches(s):
        taps = [
            x_taps[s, kw, (kh + 1) * cols : (kh + 1 + rows) * cols]
            for kh in range(3)
            for kw in range(3)
        ]
        return jnp.concatenate(taps, axis=1)

    total[:, 0:channels] = jnp.zeros((9, channels, channels), F32)
    early = dot(grad_t[0:2].reshape(2 * channels, rows * cols), patches(0))
    for tap in range(9):
        block = early[:, tap * channels : (tap + 1) * channels]
        total[tap, channels : 2 * channels] = block[:channels]
        total[tap, 2 * channels :] = block[:channels] + block[channels:]

    def weights(i, carry):
        left = [grad_t[pl.ds(PAIR * i + g, 3)].reshape(3 * channels, rows * cols) for g in range(PAIR)]
        right = [patches(PAIR * i + g) for g in range(PAIR)]
        out = dot(jnp.concatenate(left, axis=1), jnp.concatenate(right, axis=0))
        for tap in range(9):
            total[tap] += out[:, tap * channels : (tap + 1) * channels]
        return carry

    lax.fori_loop(0, frames // PAIR, weights, 0)

    def emit(low, high):
        def tap_out(tap, carry):
            at = pl.multiple_of(tap * channels, channels)
            after = pl.multiple_of((9 + tap) * channels, channels)
            low[pl.ds(at, channels), :] = total[tap, 2 * channels :].T.astype(low.dtype)
            low[pl.ds(after, channels), :] = total[tap, channels : 2 * channels].T.astype(low.dtype)
            high[pl.ds(at, channels), :] = total[tap, 0:channels].T.astype(high.dtype)
            high[pl.ds(after, channels), :] = down_total[tap].T.astype(high.dtype)
            return carry

        lax.fori_loop(0, 9, tap_out, 0)

    @pl.when(flags[5] == 0)
    def _():
        emit(kept, sent)

    @pl.when(flags[5] == 1)
    def _():
        emit(sent, kept)


def back_kernel(grad_taps, kernel_main, video_grad, w_back, total):
    frames, _, own, channels = grad_taps.shape
    inner = video_grad.shape[1]
    cols = (own - inner) // 2
    total[0:2] = jnp.zeros((2,) + total.shape[1:], F32)
    for kt in range(3):
        for tap in range(9):
            rows_at, cols_at = tap * channels, kt * channels
            block = kernel_main[9 * kt + 8 - tap].astype(F32).T.astype(BF)
            w_back[rows_at : rows_at + channels, cols_at : cols_at + channels] = block

    def group(i, carry):
        lines = []
        for t in range(GROUP):
            taps = [
                grad_taps[i * GROUP + t, kw, kh * cols : kh * cols + inner]
                for kh in range(3)
                for kw in range(3)
            ]
            lines.append(jnp.concatenate(taps, axis=1))
        out = dot(jnp.concatenate(lines, axis=0), w_back[...])
        parts = [out[:, k * channels : (k + 1) * channels] for k in range(3)]
        for g in range(GROUP):
            t, here = i * GROUP + g, slice(g * inner, (g + 1) * inner)
            total[t + 2] = parts[2][here]
            total[t + 1] += parts[1][here]
            total[t] += parts[0][here]
        return carry

    lax.fori_loop(0, frames // GROUP, group, 0)
    video_grad[0] = (total[0] + total[1] + total[2]).astype(BF)

    def store(t, carry):
        video_grad[t] = total[t + 2].astype(BF)
        return carry

    lax.fori_loop(1, frames, store, 0)


def grad_matrix(kernel_down):
    k = jnp.swapaxes(kernel_down, 2, 3)
    zero = jnp.zeros_like(k[0, 0])
    return jnp.concatenate(
        [
            jnp.concatenate([k[0, 0], zero, zero, zero], axis=1),
            jnp.concatenate([k[0, 2], k[0, 1], zero, zero], axis=1),
            jnp.concatenate([k[2, 0], zero, k[1, 0], zero], axis=1),
            jnp.concatenate([k[2, 2], k[2, 1], k[1, 2], k[1, 1]], axis=1),
        ]
    )


def on_device(video, frame_counts, kernel_main, kernel_down, latent_grad):
    _, frames, rows, cols, channels = video.shape
    ext = rows + 2
    own, outs = ext * cols, frames * rows * cols // 4
    pixels = frames * rows * cols
    vmem = pl.BlockSpec(memory_space=pltpu.VMEM)
    taps = kernel_main.reshape(27, channels, channels)

    def forward(tall):
        return pl.pallas_call(
            forward_kernel,
            out_shape=(
                jax.ShapeDtypeStruct((frames + 2, own, channels), F32),
                jax.ShapeDtypeStruct((9 * channels, 3 * channels), BF),
            ),
            in_specs=[vmem] * 2,
            out_specs=(vmem,) * 2,
            scratch_shapes=[
                pltpu.VMEM((rows + 4, cols + 16, channels), F32),
                pltpu.VMEM((GROUP, 3, (rows + 4) * cols, channels), BF),
            ],
            compiler_params=pltpu.CompilerParams(vmem_limit_bytes=16 << 20),
            cost_estimate=pl.CostEstimate(
                flops=2 * 27 * frames * own * channels * channels,
                bytes_accessed=4 << 20,
                transcendentals=0,
            ),
        )(tall, taps)

    wide, grad_wide, (pre, w_main) = with_halo(video[0], latent_grad[0], forward)
    row, col = lax.axis_index("row"), lax.axis_index("col")
    flags = jnp.stack(
        [
            frame_counts[0],
            (row > 0).astype(jnp.int32),
            (row < lax.axis_size("row") - 1).astype(jnp.int32),
            (col > 0).astype(jnp.int32),
            (col < lax.axis_size("col") - 1).astype(jnp.int32),
            lax.axis_index("clip"),
        ]
    )
    w_down = kernel_down.reshape(9 * channels, channels)
    kept, sent, grad_taps, latent = pl.pallas_call(
        main_kernel,
        out_shape=(
            jax.ShapeDtypeStruct((18 * channels, channels), F32),
            jax.ShapeDtypeStruct((18 * channels, channels), BF),
            jax.ShapeDtypeStruct((frames, 3, own, channels), BF),
            jax.ShapeDtypeStruct((outs, channels), BF),
        ),
        in_specs=[pl.BlockSpec(memory_space=pltpu.SMEM)] + [vmem] * 7,
        out_specs=(vmem,) * 4,
        scratch_shapes=[
            pltpu.VMEM((rows + 4, cols + 8, channels), F32),
            pltpu.VMEM((3, rows + 4, 2 * frames, channels), F32),
            pltpu.VMEM((frames, 3, (rows + 4) * cols, channels), BF),
            pltpu.VMEM((ext, cols, channels), F32),
            pltpu.VMEM((ext, 2 * frames, channels), F32),
            pltpu.VMEM((rows // 2 + 2, 24, channels), F32),
            pltpu.VMEM((frames, ext, cols + 16, channels), F32),
            pltpu.VMEM((ext, 2 * frames, channels), F32),
            pltpu.VMEM((ext, 2 * frames, channels), F32),
            pltpu.VMEM((ext, 2 * frames, channels), F32),
            pltpu.VMEM((ext, cols + 16, channels), F32),
            pltpu.VMEM((ext, cols + 16, channels), F32),
            pltpu.VMEM((frames, rows * cols // 4, 9 * channels), BF),
            pltpu.VMEM((frames + 2, channels, rows * cols), BF),
            pltpu.VMEM((9, 3 * channels, channels), F32),
            pltpu.VMEM((9, channels, channels), F32),
        ],
        compiler_params=pltpu.CompilerParams(vmem_limit_bytes=24 << 20),
        cost_estimate=pl.CostEstimate(
            flops=2 * 40 * pixels * channels * channels,
            bytes_accessed=12 << 20,
            transcendentals=pixels * channels,
        ),
    )(
        flags,
        wide,
        grad_wide,
        pre,
        w_main,
        grad_matrix(kernel_down),
        w_down,
        latent_grad.reshape(outs, channels),
    )
    video_grad = pl.pallas_call(
        back_kernel,
        out_shape=jax.ShapeDtypeStruct((frames, rows * cols, channels), BF),
        in_specs=[vmem] * 2,
        out_specs=vmem,
        scratch_shapes=[
            pltpu.VMEM((9 * channels, 3 * channels), BF),
            pltpu.VMEM((frames + 2, rows * cols, channels), F32),
        ],
        compiler_params=pltpu.CompilerParams(vmem_limit_bytes=12 << 20),
        cost_estimate=pl.CostEstimate(
            flops=2 * 27 * pixels * channels * channels,
            bytes_accessed=4 << 20,
            transcendentals=0,
        ),
    )(grad_taps, taps)
    main_grad, down_grad, video_grad = reduce_all(kept, sent, video_grad, 27 * channels)
    main_grad = main_grad.reshape(kernel_main.shape)
    down_grad = down_grad.reshape(kernel_down.shape)
    return (latent.reshape(latent_grad.shape), video_grad.reshape(video.shape), main_grad, down_grad)


def solution(mesh):
    tiles = P("clip", None, "row", "col", None)
    return jax.shard_map(
        on_device,
        mesh=mesh,
        in_specs=(tiles, P("clip"), P(), P(), tiles),
        out_specs=(tiles, tiles, P(), P()),
        check_vma=False,
    )
```

```python
import jax
import jax.numpy as jnp
from jax import lax
from jax.experimental import pallas as pl
from jax.experimental.pallas import tpu as pltpu
from jax.sharding import PartitionSpec as P

BF = jnp.bfloat16
F32 = jnp.float32


def flip(axis, mask):
    return [(i, i ^ mask) for i in range(lax.axis_size(axis))]


def part(x, index, size):
    return lax.dynamic_slice_in_dim(x, index * size, size, axis=0)


def exchange(low_edge, high_edge, axis):
    count = lax.axis_size(axis)
    even = lax.axis_index(axis) % 2 == 0
    inner = [(i, i ^ 1) for i in range(count - count % 2)]
    outer = [(i, ((i + 1) ^ 1) - 1) for i in range(1, count - 1 + count % 2)]
    a = lax.ppermute(jnp.where(even, high_edge, low_edge), axis, inner)
    b = lax.ppermute(jnp.where(even, low_edge, high_edge), axis, outer)
    return jnp.where(even, b, a), jnp.where(even, a, b)


def pack(a, b):
    return jnp.concatenate([a.reshape(-1, a.shape[-1]), b.reshape(-1, b.shape[-1])])


def unpack(buffer, a_shape, b_shape):
    rows = a_shape[0] * a_shape[1] * a_shape[2]
    return buffer[:rows].reshape(a_shape), buffer[rows:].reshape(b_shape)


def edges(video, grad, dim):
    size, gsize = video.shape[dim], grad.shape[dim]
    cut = lax.slice_in_dim
    low = cut(video, 0, 2, axis=dim), cut(grad, 0, 1, axis=dim)
    high = cut(video, size - 2, size, axis=dim), cut(grad, gsize - 1, gsize, axis=dim)
    return low, high


def joined(video, grad, low, high, before, after, dim):
    v_before, g_before = unpack(before, low[0].shape, low[1].shape)
    v_after, g_after = unpack(after, low[0].shape, low[1].shape)
    video = jnp.concatenate([v_before, video, v_after], axis=dim)
    return video, jnp.concatenate([g_before, grad, g_after], axis=dim)


def with_halo(video, grad, forward):
    low, high = edges(video, grad, 1)
    before, after = exchange(pack(*low), pack(*high), "row")
    tall, grad = joined(video, grad, low, high, before, after, 1)
    low, high = edges(tall, grad, 2)
    before, after = exchange(pack(*low), pack(*high), "col")
    (before, after), ready = lax.optimization_barrier(((before, after), forward(tall)))
    return joined(tall, grad, low, high, before, after, 2) + (ready,)


def combine_kernel(index, kept, got, own, *sends):
    share = own.shape[0]
    for mask in range(1 + len(sends)):
        here = pl.ds(pl.multiple_of((index[0] ^ mask) * share, share), share)
        piece = kept[here, :] + got[here, :].astype(F32)
        if mask:
            sends[mask - 1][...] = piece.astype(BF)
        else:
            own[...] = piece


def direct_scatter(kept, got, axis, beside):
    count, mine = lax.axis_size(axis), lax.axis_index(axis)
    shape = (kept.shape[0] // count, kept.shape[1])
    vmem = pl.BlockSpec(memory_space=pltpu.VMEM)
    total, *sends = pl.pallas_call(
        combine_kernel,
        out_shape=(jax.ShapeDtypeStruct(shape, F32),) + (jax.ShapeDtypeStruct(shape, BF),) * (count - 1),
        in_specs=[pl.BlockSpec(memory_space=pltpu.SMEM), vmem, vmem],
        out_specs=(vmem,) * count,
        compiler_params=pltpu.CompilerParams(vmem_limit_bytes=8 << 20),
    )(mine[None], kept, got)
    terms = [lax.ppermute(sends[mask - 1], axis, flip(axis, mask)) for mask in range(1, count)]
    terms, beside = lax.optimization_barrier((terms, beside))
    for term in terms:
        total = total + term.astype(F32)
    return total, beside


def line_sum(x, axis):
    bits, mine = lax.axis_size(axis).bit_length() - 1, lax.axis_index(axis)
    for bit in range(bits - 1):
        side, half = (mine >> bit) & 1, x.shape[0] // 2
        sent = part(x, 1 - side, half).astype(BF)
        x = part(x, side, half) + lax.ppermute(sent, axis, flip(axis, 1 << bit)).astype(F32)
    x = lax.reduce_precision(x, 8, 7)
    got = lax.ppermute(x.astype(BF), axis, flip(axis, 1 << (bits - 1)))
    y = (x + got.astype(F32)).astype(BF)
    for bit in reversed(range(bits - 1)):
        got = lax.ppermute(y, axis, flip(axis, 1 << bit))
        low = ((mine >> bit) & 1) == 0
        y = jnp.where(low, jnp.stack([y, got]), jnp.stack([got, y])).reshape(-1, y.shape[-1])
    return y


def direct_gather(y, axis):
    count, mine = lax.axis_size(axis), lax.axis_index(axis)
    share = y.shape[0]
    whole = jnp.zeros((count * share,) + y.shape[1:], y.dtype)
    whole = lax.dynamic_update_slice_in_dim(whole, y, mine * share, 0)
    for mask in range(1, count):
        got = lax.ppermute(y, axis, flip(axis, mask))
        whole = lax.dynamic_update_slice_in_dim(whole, got, (mine ^ mask) * share, 0)
    return whole


def half_kernel(which, half, *refs):
    main_grad, down_grad, turned, sems = refs[-4:]
    channels = half.shape[1]
    run = half.shape[0] // 2
    for j in range(2):
        for at in range(j * run, (j + 1) * run, channels):
            turned[at : at + channels, :] = half[at : at + channels, :].astype(F32).T
        source = turned.at[j * run : (j + 1) * run]
        for h in range(2):
            place = 2 * h + j
            target = down_grad if place == 3 else main_grad.at[place * run : (place + 1) * run]

            @pl.when(which[0] == h)
            def _():
                pltpu.make_async_copy(source, target, sems.at[j]).start()

    for j in range(2):
        source = turned.at[j * run : (j + 1) * run]
        pltpu.make_async_copy(source, down_grad, sems.at[j]).wait()


def place_half(which, half, grads, shapes):
    vmem, anywhere = (pl.BlockSpec(memory_space=m) for m in (pltpu.VMEM, pl.ANY))
    return pl.pallas_call(
        half_kernel,
        out_shape=shapes,
        in_specs=[pl.BlockSpec(memory_space=pltpu.SMEM), vmem] + [anywhere] * len(grads),
        out_specs=(anywhere, anywhere),
        input_output_aliases={2 + i: i for i in range(len(grads))},
        scratch_shapes=[pltpu.VMEM(half.shape, F32), pltpu.SemaphoreType.DMA((2,))],
        compiler_params=pltpu.CompilerParams(vmem_limit_bytes=8 << 20),
        cost_estimate=pl.CostEstimate(flops=0, bytes_accessed=4 << 20, transcendentals=0),
    )(which[None], half, *grads)


def reduce_all(kept, sent, beside, main_rows):
    half, core = kept.shape[0], lax.axis_index("clip")
    swap = flip("clip", 1)
    got = lax.ppermute(sent, "clip", swap)
    x, beside = direct_scatter(kept, got, "row", beside)
    y = direct_gather(line_sum(x, "col"), "row")
    other = lax.ppermute(y, "clip", swap)
    shapes = (
        jax.ShapeDtypeStruct((main_rows, y.shape[1]), F32),
        jax.ShapeDtypeStruct((2 * half - main_rows, y.shape[1]), F32),
    )
    grads = place_half(core, y, (), shapes)
    other, grads = lax.optimization_barrier((other, grads))
    main_grad, down_grad = place_half(1 - core, other, grads, shapes)
    return main_grad, down_grad, beside


def dot(a, b):
    return lax.dot_general(a, b, (((1,), (0,)), ((), ())), preferred_element_type=F32)


LEFT = 8


GROUP = 4
PAIR = 8


def side_by_side(kernel_main, w_main):
    channels = kernel_main.shape[1]
    for kt in range(3):
        for tap in range(9):
            rows_at, cols_at = tap * channels, kt * channels
            w_main[rows_at : rows_at + channels, cols_at : cols_at + channels] = kernel_main[9 * kt + tap]


def forward_kernel(tall, kernel_main, pre, w_main, x32, x_taps):
    frames, in_rows, cols, channels = tall.shape
    own = (in_rows - 2) * cols
    side_by_side(kernel_main, w_main)
    x32[...] = jnp.zeros_like(x32)
    for first in range(0, frames, GROUP):
        lines = []
        for g in range(GROUP):
            x32[:, LEFT : LEFT + cols, :] = tall[first + g].astype(F32)
            for kw in range(3):
                shifted = x32[:, pl.ds(LEFT - 1 + kw, cols), :].astype(BF)
                x_taps[g, kw] = shifted.reshape(in_rows * cols, channels)
            taps = [x_taps[g, kw, kh * cols : kh * cols + own] for kh in range(3) for kw in range(3)]
            lines.append(jnp.concatenate(taps, axis=1))
        out = dot(jnp.concatenate(lines, axis=0), w_main[...])
        parts = [out[:, k * channels : (k + 1) * channels] for k in range(3)]
        for g in range(GROUP):
            t, here = first + g, slice(g * own, (g + 1) * own)
            if t == 0:
                pre[0] = parts[0][here] + parts[1][here] + parts[2][here]
                pre[1] = parts[0][here] + parts[1][here]
            else:
                pre[t] += parts[2][here]
                if t + 1 < frames:
                    pre[t + 1] += parts[1][here]
            if t + 2 < frames:
                pre[t + 2] = parts[0][here]


def causal(out, channels):
    first, second, third = (out[..., k * channels : (k + 1) * channels] for k in range(3))
    frames = out.shape[-2]
    start = first[..., 0:1, :]
    back_two = jnp.concatenate([start, start, first[..., : frames - 2, :]], axis=-2)
    back_one = jnp.concatenate([second[..., 0:1, :], second[..., : frames - 1, :]], axis=-2)
    return third + back_one + back_two


def pointwise(v, grad, mask):
    logistic = 1.0 / (1.0 + jnp.exp(-v))
    out = (v * logistic * mask).astype(BF)
    back = (grad * logistic * (1.0 + v * (1.0 - logistic)) * mask).astype(BF)
    return out.astype(F32), back.astype(F32)


def main_kernel(
    flags, wide, grad_wide, pre, kernel_main, w_grad, w_down, latent_grad,
    kept, sent, own_out, side_out, latent,
    w_main, x32, side32, x_taps, v32, fix, l32, act_grad, side_back, side_act, act,
    act_taps, grad_t, total, down_total,
):
    frames, in_rows, in_cols, channels = wide.shape
    rows, cols = in_rows - 4, in_cols - 4
    ext = rows + 2
    half_rows, half_cols = rows // 2, cols // 2
    own = ext * cols
    grad_t[frames:] = jnp.zeros((2,) + grad_t.shape[1:], BF)
    l32[...] = jnp.zeros_like(l32)
    side_by_side(kernel_main, w_main)
    count = flags[0]
    low_row, high_row = flags[1].astype(F32), flags[2].astype(F32)
    low_col, high_col = flags[3].astype(F32), flags[4].astype(F32)

    def spread(t, carry):
        x32[:, 0:in_cols, :] = wide[t].astype(F32)
        for kw in range(3):
            shifted = x32[:, pl.ds(1 + kw, cols), :].astype(BF)
            x_taps[t, kw] = shifted.reshape(in_rows * cols, channels)
            side32[kw, :, pl.ds(t, 1), :] = x32[:, kw : kw + 1, :]
            side32[kw, :, pl.ds(frames + t, 1), :] = x32[:, cols + 1 + kw : cols + 2 + kw, :]
        l32[:, 0 : half_cols + 2, :] = grad_wide[t].astype(F32)
        near = [l32[:, pl.ds(dq, 16), :].astype(BF) for dq in range(2)]
        grads = jnp.concatenate(
            [
                near[dq][dp : dp + half_rows + 1].reshape((half_rows + 1) * 16, channels)
                for dp in (1, 0)
                for dq in (1, 0)
            ],
            axis=1,
        )
        classes = dot(grads, w_grad[...])
        for p in range(half_rows + 1):
            for odd in range(2):
                line = classes[p * 16 : p * 16 + half_cols + 1]
                row = 2 * p + 1 - odd
                even_part = line[:, 2 * odd * channels : (2 * odd + 1) * channels]
                odd_part = line[:, (2 * odd + 1) * channels : (2 * odd + 2) * channels]
                act_grad[t, row, pl.ds(LEFT, half_cols + 1, stride=2), :] = even_part
                act_grad[t, row, pl.ds(LEFT - 1, half_cols + 1, stride=2), :] = odd_part
        side_back[:, pl.ds(t, 1), :] = act_grad[t, :, LEFT - 1 : LEFT, :]
        side_back[:, pl.ds(frames + t, 1), :] = act_grad[t, :, LEFT + cols : LEFT + cols + 1, :]
        return carry

    lax.fori_loop(0, frames, spread, 0)

    side_lhs = jnp.concatenate(
        [
            side32[kw, kh : kh + ext].reshape(ext * 2 * frames, channels).astype(BF)
            for kh in range(3)
            for kw in range(3)
        ],
        axis=1,
    )
    side_pre = dot(side_lhs, w_main[...]).reshape(ext, 2, frames, 3 * channels)
    side_pre = causal(side_pre, channels).reshape(ext, 2 * frames, channels)
    for side in range(2):
        at = side * frames
        lhs = jnp.concatenate(
            [
                side32[1, kh : kh + ext, at : at + frames].reshape(ext * frames, channels).astype(BF)
                for kh in range(3)
            ],
            axis=1,
        )
        weights_here = jnp.concatenate(
            [
                w_main[(3 * kh + 2 * side) * channels : (3 * kh + 2 * side + 1) * channels]
                for kh in range(3)
            ],
            axis=0,
        )
        out = dot(lhs, weights_here).reshape(ext, frames, 3 * channels)
        fix[:, at : at + frames, :] = causal(out, channels)

    def row_mask(width):
        place = lax.broadcasted_iota(jnp.int32, (ext, width, channels), 0)
        return jnp.where(place == 0, low_row, jnp.where(place == ext - 1, high_row, 1.0))

    place = lax.broadcasted_iota(jnp.int32, (ext, 2 * frames, channels), 1)
    side_mask = jnp.where(place < frames, low_col, high_col)
    side_mask = jnp.where(place % frames < count, side_mask, 0.0) * row_mask(2 * frames)
    side_act[...], side_grad = pointwise(side_pre, side_back[...], side_mask)
    side_out[...] = side_grad.astype(BF)

    def frame(t, carry):
        live = jnp.where(t < count, 1.0, 0.0).astype(F32)
        last = frames + t
        v32[...] = pre[t].reshape(ext, cols, channels)
        v32[:, 0:1, :] += fix[:, pl.ds(t, 1), :]
        v32[:, cols - 1 : cols, :] += fix[:, pl.ds(last, 1), :]
        own_act, own_grad = pointwise(
            v32[...], act_grad[t, :, LEFT : LEFT + cols, :], row_mask(cols) * live
        )
        act[:, LEFT : LEFT + cols, :] = own_act
        act[:, LEFT + cols : LEFT + cols + 1, :] = side_act[:, pl.ds(last, 1), :]
        own_out[t] = own_grad.reshape(own, channels).astype(BF)
        inner = own_grad.reshape(own, channels)[cols : cols + rows * cols]
        grad_t[t] = inner.T.astype(BF)
        for a in range(3):
            for b in range(3):
                tap = jnp.concatenate(
                    [
                        act[2 * i + a + 1, pl.ds(LEFT + b, half_cols, stride=2), :]
                        for i in range(half_rows)
                    ],
                    axis=0,
                ).astype(BF)
                at = (3 * a + b) * channels
                act_taps[t, :, at : at + channels] = tap
        return carry

    lax.fori_loop(0, frames, frame, 0)

    flat = act_taps[...].reshape(frames * half_rows * half_cols, 9 * channels)
    latent[...] = dot(flat, w_down[...]).astype(BF)
    down = dot(latent_grad[...].astype(F32).T.astype(BF), flat)
    for tap in range(9):
        down_total[tap] = down[:, tap * channels : (tap + 1) * channels]

    def patches(s):
        taps = [
            x_taps[s, kw, (kh + 1) * cols : (kh + 1 + rows) * cols]
            for kh in range(3)
            for kw in range(3)
        ]
        return jnp.concatenate(taps, axis=1)

    total[:, 0:channels] = jnp.zeros((9, channels, channels), F32)
    early = dot(grad_t[0:2].reshape(2 * channels, rows * cols), patches(0))
    for tap in range(9):
        block = early[:, tap * channels : (tap + 1) * channels]
        total[tap, channels : 2 * channels] = block[:channels]
        total[tap, 2 * channels :] = block[:channels] + block[channels:]

    def weights(i, carry):
        left = [grad_t[pl.ds(PAIR * i + g, 3)].reshape(3 * channels, rows * cols) for g in range(PAIR)]
        right = [patches(PAIR * i + g) for g in range(PAIR)]
        out = dot(jnp.concatenate(left, axis=1), jnp.concatenate(right, axis=0))
        for tap in range(9):
            total[tap] += out[:, tap * channels : (tap + 1) * channels]
        return carry

    lax.fori_loop(0, frames // PAIR, weights, 0)

    def emit(low, high):
        def tap_out(tap, carry):
            at = pl.multiple_of(tap * channels, channels)
            after = pl.multiple_of((9 + tap) * channels, channels)
            low[pl.ds(at, channels), :] = total[tap, 2 * channels :].astype(low.dtype)
            low[pl.ds(after, channels), :] = total[tap, channels : 2 * channels].astype(low.dtype)
            high[pl.ds(at, channels), :] = total[tap, 0:channels].astype(high.dtype)
            high[pl.ds(after, channels), :] = down_total[tap].astype(high.dtype)
            return carry

        lax.fori_loop(0, 9, tap_out, 0)

    @pl.when(flags[5] == 0)
    def _():
        emit(kept, sent)

    @pl.when(flags[5] == 1)
    def _():
        emit(sent, kept)


def back_kernel(own_grad, side_grad, kernel_main, video_grad, w_back, total, side32, g32, grad_taps):
    frames, own, channels = own_grad.shape
    inner = video_grad.shape[1]
    cols = (own - inner) // 2
    ext = own // cols
    side32[...] = side_grad[...].astype(F32)
    total[0:2] = jnp.zeros((2,) + total.shape[1:], F32)
    for kt in range(3):
        for tap in range(9):
            rows_at, cols_at = tap * channels, kt * channels
            block = kernel_main[9 * kt + 8 - tap].astype(F32).T.astype(BF)
            w_back[rows_at : rows_at + channels, cols_at : cols_at + channels] = block

    def group(i, carry):
        lines = []
        for g in range(GROUP):
            t = i * GROUP + g
            g32[:, LEFT : LEFT + cols, :] = own_grad[t].astype(F32).reshape(ext, cols, channels)
            g32[:, LEFT - 1 : LEFT, :] = side32[:, pl.ds(t, 1), :]
            g32[:, LEFT + cols : LEFT + cols + 1, :] = side32[:, pl.ds(frames + t, 1), :]
            for kw in range(3):
                shifted = g32[:, pl.ds(LEFT - 1 + kw, cols), :].astype(BF)
                grad_taps[g, kw] = shifted.reshape(own, channels)
            taps = [
                grad_taps[g, kw, kh * cols : kh * cols + inner]
                for kh in range(3)
                for kw in range(3)
            ]
            lines.append(jnp.concatenate(taps, axis=1))
        out = dot(jnp.concatenate(lines, axis=0), w_back[...])
        parts = [out[:, k * channels : (k + 1) * channels] for k in range(3)]
        for g in range(GROUP):
            t, here = i * GROUP + g, slice(g * inner, (g + 1) * inner)
            total[t + 2] = parts[2][here]
            total[t + 1] += parts[1][here]
            total[t] += parts[0][here]
        return carry

    lax.fori_loop(0, frames // GROUP, group, 0)
    video_grad[0] = (total[0] + total[1] + total[2]).astype(BF)

    def store(t, carry):
        video_grad[t] = total[t + 2].astype(BF)
        return carry

    lax.fori_loop(1, frames, store, 0)


def grad_matrix(kernel_down):
    k = jnp.swapaxes(kernel_down, 2, 3)
    zero = jnp.zeros_like(k[0, 0])
    return jnp.concatenate(
        [
            jnp.concatenate([k[0, 0], zero, zero, zero], axis=1),
            jnp.concatenate([k[0, 2], k[0, 1], zero, zero], axis=1),
            jnp.concatenate([k[2, 0], zero, k[1, 0], zero], axis=1),
            jnp.concatenate([k[2, 2], k[2, 1], k[1, 2], k[1, 1]], axis=1),
        ]
    )


def on_device(video, frame_counts, kernel_main, kernel_down, latent_grad):
    _, frames, rows, cols, channels = video.shape
    ext = rows + 2
    own, outs = ext * cols, frames * rows * cols // 4
    pixels = frames * rows * cols
    vmem = pl.BlockSpec(memory_space=pltpu.VMEM)
    taps = kernel_main.reshape(27, channels, channels)

    def forward(tall):
        return pl.pallas_call(
            forward_kernel,
            out_shape=(
                jax.ShapeDtypeStruct((frames, own, channels), F32),
            ),
            in_specs=[vmem] * 2,
            out_specs=(vmem,),
            scratch_shapes=[
                pltpu.VMEM((9 * channels, 3 * channels), BF),
                pltpu.VMEM((rows + 4, cols + 16, channels), F32),
                pltpu.VMEM((GROUP, 3, (rows + 4) * cols, channels), BF),
            ],
            compiler_params=pltpu.CompilerParams(vmem_limit_bytes=16 << 20),
            cost_estimate=pl.CostEstimate(
                flops=2 * 27 * frames * own * channels * channels,
                bytes_accessed=4 << 20,
                transcendentals=0,
            ),
        )(tall, taps)

    wide, grad_wide, (pre,) = with_halo(video[0], latent_grad[0], forward)
    row, col = lax.axis_index("row"), lax.axis_index("col")
    flags = jnp.stack(
        [
            frame_counts[0],
            (row > 0).astype(jnp.int32),
            (row < lax.axis_size("row") - 1).astype(jnp.int32),
            (col > 0).astype(jnp.int32),
            (col < lax.axis_size("col") - 1).astype(jnp.int32),
            lax.axis_index("clip"),
        ]
    )
    w_down = kernel_down.reshape(9 * channels, channels)
    kept, sent, own_grad, side_grad, latent = pl.pallas_call(
        main_kernel,
        out_shape=(
            jax.ShapeDtypeStruct((18 * channels, channels), F32),
            jax.ShapeDtypeStruct((18 * channels, channels), BF),
            jax.ShapeDtypeStruct((frames, own, channels), BF),
            jax.ShapeDtypeStruct((ext, 2 * frames, channels), BF),
            jax.ShapeDtypeStruct((outs, channels), BF),
        ),
        in_specs=[pl.BlockSpec(memory_space=pltpu.SMEM)] + [vmem] * 7,
        out_specs=(vmem,) * 5,
        scratch_shapes=[
            pltpu.VMEM((9 * channels, 3 * channels), BF),
            pltpu.VMEM((rows + 4, cols + 8, channels), F32),
            pltpu.VMEM((3, rows + 4, 2 * frames, channels), F32),
            pltpu.VMEM((frames, 3, (rows + 4) * cols, channels), BF),
            pltpu.VMEM((ext, cols, channels), F32),
            pltpu.VMEM((ext, 2 * frames, channels), F32),
            pltpu.VMEM((rows // 2 + 2, 24, channels), F32),
            pltpu.VMEM((frames, ext, cols + 16, channels), F32),
            pltpu.VMEM((ext, 2 * frames, channels), F32),
            pltpu.VMEM((ext, 2 * frames, channels), F32),
            pltpu.VMEM((ext, cols + 16, channels), F32),
            pltpu.VMEM((frames, rows * cols // 4, 9 * channels), BF),
            pltpu.VMEM((frames + 2, channels, rows * cols), BF),
            pltpu.VMEM((9, 3 * channels, channels), F32),
            pltpu.VMEM((9, channels, channels), F32),
        ],
        compiler_params=pltpu.CompilerParams(vmem_limit_bytes=24 << 20),
        cost_estimate=pl.CostEstimate(
            flops=2 * 40 * pixels * channels * channels,
            bytes_accessed=12 << 20,
            transcendentals=pixels * channels,
        ),
    )(
        flags,
        wide,
        grad_wide,
        pre,
        taps,
        grad_matrix(kernel_down),
        w_down,
        latent_grad.reshape(outs, channels),
    )
    video_grad = pl.pallas_call(
        back_kernel,
        out_shape=jax.ShapeDtypeStruct((frames, rows * cols, channels), BF),
        in_specs=[vmem] * 3,
        out_specs=vmem,
        scratch_shapes=[
            pltpu.VMEM((9 * channels, 3 * channels), BF),
            pltpu.VMEM((frames + 2, rows * cols, channels), F32),
            pltpu.VMEM((ext, 2 * frames, channels), F32),
            pltpu.VMEM((ext, cols + 16, channels), F32),
            pltpu.VMEM((GROUP, 3, own, channels), BF),
        ],
        compiler_params=pltpu.CompilerParams(vmem_limit_bytes=12 << 20),
        cost_estimate=pl.CostEstimate(
            flops=2 * 27 * pixels * channels * channels,
            bytes_accessed=4 << 20,
            transcendentals=0,
        ),
    )(own_grad, side_grad, taps)
    main_grad, down_grad, video_grad = reduce_all(kept, sent, video_grad, 27 * channels)
    main_grad = main_grad.reshape(kernel_main.shape)
    down_grad = down_grad.reshape(kernel_down.shape)
    return (latent.reshape(latent_grad.shape), video_grad.reshape(video.shape), main_grad, down_grad)


def solution(mesh):
    tiles = P("clip", None, "row", "col", None)
    return jax.shard_map(
        on_device,
        mesh=mesh,
        in_specs=(tiles, P("clip"), P(), P(), tiles),
        out_specs=(tiles, tiles, P(), P()),
        check_vma=False,
    )
```

```python
import jax
import jax.numpy as jnp
from jax import lax
from jax.experimental import pallas as pl
from jax.experimental.pallas import tpu as pltpu
from jax.sharding import PartitionSpec as P

BF = jnp.bfloat16
F32 = jnp.float32


def flip(axis, mask):
    return [(i, i ^ mask) for i in range(lax.axis_size(axis))]


def part(x, index, size):
    return lax.dynamic_slice_in_dim(x, index * size, size, axis=0)


def exchange(low_edge, high_edge, axis):
    count = lax.axis_size(axis)
    even = lax.axis_index(axis) % 2 == 0
    inner = [(i, i ^ 1) for i in range(count - count % 2)]
    outer = [(i, ((i + 1) ^ 1) - 1) for i in range(1, count - 1 + count % 2)]
    a = lax.ppermute(jnp.where(even, high_edge, low_edge), axis, inner)
    b = lax.ppermute(jnp.where(even, low_edge, high_edge), axis, outer)
    return jnp.where(even, b, a), jnp.where(even, a, b)


def pack(a, b):
    return jnp.concatenate([a.reshape(-1, a.shape[-1]), b.reshape(-1, b.shape[-1])])


def unpack(buffer, a_shape, b_shape):
    rows = a_shape[0] * a_shape[1] * a_shape[2]
    return buffer[:rows].reshape(a_shape), buffer[rows:].reshape(b_shape)


def edges(video, grad, dim):
    size, gsize = video.shape[dim], grad.shape[dim]
    cut = lax.slice_in_dim
    low = cut(video, 0, 2, axis=dim), cut(grad, 0, 1, axis=dim)
    high = cut(video, size - 2, size, axis=dim), cut(grad, gsize - 1, gsize, axis=dim)
    return low, high


def joined(video, grad, low, high, before, after, dim):
    v_before, g_before = unpack(before, low[0].shape, low[1].shape)
    v_after, g_after = unpack(after, low[0].shape, low[1].shape)
    video = jnp.concatenate([v_before, video, v_after], axis=dim)
    return video, jnp.concatenate([g_before, grad, g_after], axis=dim)


def with_halo(video, grad, forward):
    low, high = edges(video, grad, 1)
    before, after = exchange(pack(*low), pack(*high), "row")
    tall, grad = joined(video, grad, low, high, before, after, 1)
    low, high = edges(tall, grad, 2)
    before, after = exchange(pack(*low), pack(*high), "col")
    (before, after), ready = lax.optimization_barrier(((before, after), forward(tall)))
    return joined(tall, grad, low, high, before, after, 2) + (ready,)


def combine_kernel(index, kept, got, own, *sends):
    share = own.shape[0]
    for mask in range(1 + len(sends)):
        here = pl.ds(pl.multiple_of((index[0] ^ mask) * share, share), share)
        piece = kept[here, :] + got[here, :].astype(F32)
        if mask:
            sends[mask - 1][...] = piece.astype(BF)
        else:
            own[...] = piece


def direct_scatter(kept, got, axis, beside):
    count, mine = lax.axis_size(axis), lax.axis_index(axis)
    shape = (kept.shape[0] // count, kept.shape[1])
    vmem = pl.BlockSpec(memory_space=pltpu.VMEM)
    total, *sends = pl.pallas_call(
        combine_kernel,
        out_shape=(jax.ShapeDtypeStruct(shape, F32),) + (jax.ShapeDtypeStruct(shape, BF),) * (count - 1),
        in_specs=[pl.BlockSpec(memory_space=pltpu.SMEM), vmem, vmem],
        out_specs=(vmem,) * count,
        compiler_params=pltpu.CompilerParams(vmem_limit_bytes=8 << 20),
    )(mine[None], kept, got)
    order = range(count - 1, 0, -1)
    terms = [lax.ppermute(sends[mask - 1], axis, flip(axis, mask)) for mask in order]
    terms, beside = lax.optimization_barrier((terms, beside))
    for term in terms:
        total = total + term.astype(F32)
    return total, beside


def line_sum(x, axis):
    bits, mine = lax.axis_size(axis).bit_length() - 1, lax.axis_index(axis)
    for bit in range(bits - 1):
        side, half = (mine >> bit) & 1, x.shape[0] // 2
        sent = part(x, 1 - side, half).astype(BF)
        x = part(x, side, half) + lax.ppermute(sent, axis, flip(axis, 1 << bit)).astype(F32)
    x = lax.reduce_precision(x, 8, 7)
    got = lax.ppermute(x.astype(BF), axis, flip(axis, 1 << (bits - 1)))
    y = (x + got.astype(F32)).astype(BF)
    for bit in reversed(range(bits - 1)):
        got = lax.ppermute(y, axis, flip(axis, 1 << bit))
        low = ((mine >> bit) & 1) == 0
        y = jnp.where(low, jnp.stack([y, got]), jnp.stack([got, y])).reshape(-1, y.shape[-1])
    return y


def direct_gather(y, axis):
    count, mine = lax.axis_size(axis), lax.axis_index(axis)
    share = y.shape[0]
    whole = jnp.zeros((count * share,) + y.shape[1:], y.dtype)
    whole = lax.dynamic_update_slice_in_dim(whole, y, mine * share, 0)
    for mask in range(count - 1, 0, -1):
        got = lax.ppermute(y, axis, flip(axis, mask))
        whole = lax.dynamic_update_slice_in_dim(whole, got, (mine ^ mask) * share, 0)
    return whole


def half_kernel(which, half, *refs):
    main_grad, down_grad, turned, sems = refs[-4:]
    channels = half.shape[1]
    run = half.shape[0] // 2
    for j in range(2):
        for at in range(j * run, (j + 1) * run, channels):
            turned[at : at + channels, :] = half[at : at + channels, :].astype(F32).T
        source = turned.at[j * run : (j + 1) * run]
        for h in range(2):
            place = 2 * h + j
            target = down_grad if place == 3 else main_grad.at[place * run : (place + 1) * run]

            @pl.when(which[0] == h)
            def _():
                pltpu.make_async_copy(source, target, sems.at[j]).start()

    for j in range(2):
        source = turned.at[j * run : (j + 1) * run]
        pltpu.make_async_copy(source, down_grad, sems.at[j]).wait()


def place_half(which, half, grads, shapes):
    vmem, anywhere = (pl.BlockSpec(memory_space=m) for m in (pltpu.VMEM, pl.ANY))
    return pl.pallas_call(
        half_kernel,
        out_shape=shapes,
        in_specs=[pl.BlockSpec(memory_space=pltpu.SMEM), vmem] + [anywhere] * len(grads),
        out_specs=(anywhere, anywhere),
        input_output_aliases={2 + i: i for i in range(len(grads))},
        scratch_shapes=[pltpu.VMEM(half.shape, F32), pltpu.SemaphoreType.DMA((2,))],
        compiler_params=pltpu.CompilerParams(vmem_limit_bytes=8 << 20),
        cost_estimate=pl.CostEstimate(flops=0, bytes_accessed=4 << 20, transcendentals=0),
    )(which[None], half, *grads)


def reduce_all(kept, sent, beside, main_rows):
    half, core = kept.shape[0], lax.axis_index("clip")
    swap = flip("clip", 1)
    got = lax.ppermute(sent, "clip", swap)
    x, beside = direct_scatter(kept, got, "row", beside)
    y = direct_gather(line_sum(x, "col"), "row")
    other = lax.ppermute(y, "clip", swap)
    shapes = (
        jax.ShapeDtypeStruct((main_rows, y.shape[1]), F32),
        jax.ShapeDtypeStruct((2 * half - main_rows, y.shape[1]), F32),
    )
    grads = place_half(core, y, (), shapes)
    other, grads = lax.optimization_barrier((other, grads))
    main_grad, down_grad = place_half(1 - core, other, grads, shapes)
    return main_grad, down_grad, beside


def dot(a, b):
    return lax.dot_general(a, b, (((1,), (0,)), ((), ())), preferred_element_type=F32)


LEFT = 8


GROUP = 4


def side_by_side(kernel_main, w_main):
    channels = kernel_main.shape[1]
    for kt in range(3):
        for tap in range(9):
            rows_at, cols_at = tap * channels, kt * channels
            w_main[rows_at : rows_at + channels, cols_at : cols_at + channels] = kernel_main[9 * kt + tap]


def forward_kernel(tall, kernel_main, pre, w_main, x32, x_taps):
    frames, in_rows, cols, channels = tall.shape
    own = (in_rows - 2) * cols
    side_by_side(kernel_main, w_main)
    x32[...] = jnp.zeros_like(x32)
    for first in range(0, frames, GROUP):
        lines = []
        for g in range(GROUP):
            x32[:, LEFT : LEFT + cols, :] = tall[first + g].astype(F32)
            for kw in range(3):
                shifted = x32[:, pl.ds(LEFT - 1 + kw, cols), :].astype(BF)
                x_taps[g, kw] = shifted.reshape(in_rows * cols, channels)
            taps = [x_taps[g, kw, kh * cols : kh * cols + own] for kh in range(3) for kw in range(3)]
            lines.append(jnp.concatenate(taps, axis=1))
        out = dot(jnp.concatenate(lines, axis=0), w_main[...])
        parts = [out[:, k * channels : (k + 1) * channels] for k in range(3)]
        for g in range(GROUP):
            t, here = first + g, slice(g * own, (g + 1) * own)
            if t == 0:
                pre[0] = parts[0][here] + parts[1][here] + parts[2][here]
                pre[1] = parts[0][here] + parts[1][here]
            else:
                pre[t] += parts[2][here]
                if t + 1 < frames:
                    pre[t + 1] += parts[1][here]
            if t + 2 < frames:
                pre[t + 2] = parts[0][here]


def causal(out, channels):
    first, second, third = (out[..., k * channels : (k + 1) * channels] for k in range(3))
    frames = out.shape[-2]
    start = first[..., 0:1, :]
    back_two = jnp.concatenate([start, start, first[..., : frames - 2, :]], axis=-2)
    back_one = jnp.concatenate([second[..., 0:1, :], second[..., : frames - 1, :]], axis=-2)
    return third + back_one + back_two


def pointwise(v, grad, mask):
    logistic = 1.0 / (1.0 + jnp.exp(-v))
    out = (v * logistic * mask).astype(BF)
    back = (grad * logistic * (1.0 + v * (1.0 - logistic)) * mask).astype(BF)
    return out.astype(F32), back.astype(F32)


def main_kernel(
    flags, wide, grad_wide, pre, kernel_main, w_grad, w_down, latent_grad,
    kept, sent, own_out, side_out, latent,
    w_main, x32, side32, x_taps, v32, fix, l32, act_grad, side_back, side_act, act,
    act_taps, grad_t, total, down_total,
):
    frames, in_rows, in_cols, channels = wide.shape
    rows, cols = in_rows - 4, in_cols - 4
    ext = rows + 2
    half_rows, half_cols = rows // 2, cols // 2
    own = ext * cols
    grad_t[frames:] = jnp.zeros((2,) + grad_t.shape[1:], BF)
    l32[...] = jnp.zeros_like(l32)
    side_by_side(kernel_main, w_main)
    count = flags[0]
    low_row, high_row = flags[1].astype(F32), flags[2].astype(F32)
    low_col, high_col = flags[3].astype(F32), flags[4].astype(F32)

    def spread(i, carry):
        lines = []
        for g in range(GROUP):
            t = i * GROUP + g
            x32[:, 0:in_cols, :] = wide[t].astype(F32)
            for kw in range(3):
                shifted = x32[:, pl.ds(1 + kw, cols), :].astype(BF)
                x_taps[t, kw] = shifted.reshape(in_rows * cols, channels)
                side32[kw, :, pl.ds(t, 1), :] = x32[:, kw : kw + 1, :]
                side32[kw, :, pl.ds(frames + t, 1), :] = x32[:, cols + 1 + kw : cols + 2 + kw, :]
            l32[:, 0 : half_cols + 2, :] = grad_wide[t].astype(F32)
            near = [l32[:, pl.ds(dq, 16), :].astype(BF) for dq in range(2)]
            shifts = [
                near[dq][dp : dp + half_rows + 1].reshape((half_rows + 1) * 16, channels)
                for dp in (1, 0)
                for dq in (1, 0)
            ]
            lines.append(jnp.concatenate(shifts, axis=1))
        classes = dot(jnp.concatenate(lines, axis=0), w_grad[...])
        for g in range(GROUP):
            t = i * GROUP + g
            for p in range(half_rows + 1):
                at = (g * (half_rows + 1) + p) * 16
                for odd in range(2):
                    line = classes[at : at + half_cols + 1]
                    row = 2 * p + 1 - odd
                    even_part = line[:, 2 * odd * channels : (2 * odd + 1) * channels]
                    odd_part = line[:, (2 * odd + 1) * channels : (2 * odd + 2) * channels]
                    act_grad[t, row, pl.ds(LEFT, half_cols + 1, stride=2), :] = even_part
                    act_grad[t, row, pl.ds(LEFT - 1, half_cols + 1, stride=2), :] = odd_part
            side_back[:, pl.ds(t, 1), :] = act_grad[t, :, LEFT - 1 : LEFT, :]
            side_back[:, pl.ds(frames + t, 1), :] = act_grad[t, :, LEFT + cols : LEFT + cols + 1, :]
        return carry

    lax.fori_loop(0, frames // GROUP, spread, 0)

    side_lhs = jnp.concatenate(
        [
            side32[kw, kh : kh + ext].reshape(ext * 2 * frames, channels).astype(BF)
            for kh in range(3)
            for kw in range(3)
        ],
        axis=1,
    )
    side_pre = dot(side_lhs, w_main[...]).reshape(ext, 2, frames, 3 * channels)
    side_pre = causal(side_pre, channels).reshape(ext, 2 * frames, channels)
    for side in range(2):
        at = side * frames
        lhs = jnp.concatenate(
            [
                side32[1, kh : kh + ext, at : at + frames].reshape(ext * frames, channels).astype(BF)
                for kh in range(3)
            ],
            axis=1,
        )
        weights_here = jnp.concatenate(
            [
                w_main[(3 * kh + 2 * side) * channels : (3 * kh + 2 * side + 1) * channels]
                for kh in range(3)
            ],
            axis=0,
        )
        out = dot(lhs, weights_here).reshape(ext, frames, 3 * channels)
        fix[:, at : at + frames, :] = causal(out, channels)

    def row_mask(width):
        place = lax.broadcasted_iota(jnp.int32, (ext, width, channels), 0)
        return jnp.where(place == 0, low_row, jnp.where(place == ext - 1, high_row, 1.0))

    place = lax.broadcasted_iota(jnp.int32, (ext, 2 * frames, channels), 1)
    side_mask = jnp.where(place < frames, low_col, high_col)
    side_mask = jnp.where(place % frames < count, side_mask, 0.0) * row_mask(2 * frames)
    side_act[...], side_grad = pointwise(side_pre, side_back[...], side_mask)
    side_out[...] = side_grad.astype(BF)

    def frame(t, carry):
        live = jnp.where(t < count, 1.0, 0.0).astype(F32)
        last = frames + t
        v32[...] = pre[t].reshape(ext, cols, channels)
        v32[:, 0:1, :] += fix[:, pl.ds(t, 1), :]
        v32[:, cols - 1 : cols, :] += fix[:, pl.ds(last, 1), :]
        own_act, own_grad = pointwise(
            v32[...], act_grad[t, :, LEFT : LEFT + cols, :], row_mask(cols) * live
        )
        act[:, LEFT : LEFT + cols, :] = own_act
        act[:, LEFT + cols : LEFT + cols + 1, :] = side_act[:, pl.ds(last, 1), :]
        own_out[t] = own_grad.reshape(own, channels).astype(BF)
        inner = own_grad.reshape(own, channels)[cols : cols + rows * cols]
        grad_t[t] = inner.T.astype(BF)
        for a in range(3):
            for b in range(3):
                tap = jnp.concatenate(
                    [
                        act[2 * i + a + 1, pl.ds(LEFT + b, half_cols, stride=2), :]
                        for i in range(half_rows)
                    ],
                    axis=0,
                ).astype(BF)
                at = (3 * a + b) * channels
                act_taps[t, :, at : at + channels] = tap
        return carry

    lax.fori_loop(0, frames, frame, 0)

    flat = act_taps[...].reshape(frames * half_rows * half_cols, 9 * channels)
    latent[...] = dot(flat, w_down[...]).astype(BF)
    down = dot(latent_grad[...].astype(F32).T.astype(BF), flat)
    for tap in range(9):
        down_total[tap] = down[:, tap * channels : (tap + 1) * channels]

    def patches(s):
        taps = [
            x_taps[s, kw, (kh + 1) * cols : (kh + 1 + rows) * cols]
            for kh in range(3)
            for kw in range(3)
        ]
        return jnp.concatenate(taps, axis=1)

    early = dot(grad_t[0:2].reshape(2 * channels, rows * cols), patches(0))
    for tap in range(9):
        block = early[:, tap * channels : (tap + 1) * channels]
        total[tap, 0:channels] = block[:channels]
        total[tap, channels:] = block[:channels] + block[channels:]

    left = [grad_t[t : t + 3].reshape(3 * channels, rows * cols) for t in range(frames)]
    right = [patches(t) for t in range(frames)]
    out = dot(jnp.concatenate(left, axis=1), jnp.concatenate(right, axis=0))

    def emit(low, high):
        for tap in range(9):
            at, after = tap * channels, (9 + tap) * channels
            block = out[:, tap * channels : (tap + 1) * channels]
            first, second, third = (block[k * channels : (k + 1) * channels] for k in (2, 1, 0))
            low[at : at + channels, :] = (first + total[tap, channels:]).astype(low.dtype)
            low[after : after + channels, :] = (second + total[tap, 0:channels]).astype(low.dtype)
            high[at : at + channels, :] = third.astype(high.dtype)
            high[after : after + channels, :] = down_total[tap].astype(high.dtype)

    @pl.when(flags[5] == 0)
    def _():
        emit(kept, sent)

    @pl.when(flags[5] == 1)
    def _():
        emit(sent, kept)


def back_kernel(own_grad, side_grad, kernel_main, video_grad, w_back, total, side32, g32, grad_taps):
    frames, own, channels = own_grad.shape
    inner = video_grad.shape[1]
    cols = (own - inner) // 2
    ext = own // cols
    side32[...] = side_grad[...].astype(F32)
    total[0:2] = jnp.zeros((2,) + total.shape[1:], F32)
    for kt in range(3):
        for tap in range(9):
            rows_at, cols_at = tap * channels, kt * channels
            block = kernel_main[9 * kt + 8 - tap].astype(F32).T.astype(BF)
            w_back[rows_at : rows_at + channels, cols_at : cols_at + channels] = block

    def group(i, carry):
        lines = []
        for g in range(GROUP):
            t = i * GROUP + g
            g32[:, LEFT : LEFT + cols, :] = own_grad[t].astype(F32).reshape(ext, cols, channels)
            g32[:, LEFT - 1 : LEFT, :] = side32[:, pl.ds(t, 1), :]
            g32[:, LEFT + cols : LEFT + cols + 1, :] = side32[:, pl.ds(frames + t, 1), :]
            for kw in range(3):
                shifted = g32[:, pl.ds(LEFT - 1 + kw, cols), :].astype(BF)
                grad_taps[g, kw] = shifted.reshape(own, channels)
            taps = [
                grad_taps[g, kw, kh * cols : kh * cols + inner]
                for kh in range(3)
                for kw in range(3)
            ]
            lines.append(jnp.concatenate(taps, axis=1))
        out = dot(jnp.concatenate(lines, axis=0), w_back[...])
        parts = [out[:, k * channels : (k + 1) * channels] for k in range(3)]
        for g in range(GROUP):
            t, here = i * GROUP + g, slice(g * inner, (g + 1) * inner)
            total[t + 2] = parts[2][here]
            total[t + 1] += parts[1][here]
            total[t] += parts[0][here]
        return carry

    lax.fori_loop(0, frames // GROUP, group, 0)
    video_grad[0] = (total[0] + total[1] + total[2]).astype(BF)

    def store(t, carry):
        video_grad[t] = total[t + 2].astype(BF)
        return carry

    lax.fori_loop(1, frames, store, 0)


def grad_matrix(kernel_down):
    k = jnp.swapaxes(kernel_down, 2, 3)
    zero = jnp.zeros_like(k[0, 0])
    return jnp.concatenate(
        [
            jnp.concatenate([k[0, 0], zero, zero, zero], axis=1),
            jnp.concatenate([k[0, 2], k[0, 1], zero, zero], axis=1),
            jnp.concatenate([k[2, 0], zero, k[1, 0], zero], axis=1),
            jnp.concatenate([k[2, 2], k[2, 1], k[1, 2], k[1, 1]], axis=1),
        ]
    )


def on_device(video, frame_counts, kernel_main, kernel_down, latent_grad):
    _, frames, rows, cols, channels = video.shape
    ext = rows + 2
    own, outs = ext * cols, frames * rows * cols // 4
    pixels = frames * rows * cols
    vmem = pl.BlockSpec(memory_space=pltpu.VMEM)
    taps = kernel_main.reshape(27, channels, channels)

    def forward(tall):
        return pl.pallas_call(
            forward_kernel,
            out_shape=(
                jax.ShapeDtypeStruct((frames, own, channels), F32),
            ),
            in_specs=[vmem] * 2,
            out_specs=(vmem,),
            scratch_shapes=[
                pltpu.VMEM((9 * channels, 3 * channels), BF),
                pltpu.VMEM((rows + 4, cols + 16, channels), F32),
                pltpu.VMEM((GROUP, 3, (rows + 4) * cols, channels), BF),
            ],
            compiler_params=pltpu.CompilerParams(vmem_limit_bytes=16 << 20),
            cost_estimate=pl.CostEstimate(
                flops=2 * 27 * frames * own * channels * channels,
                bytes_accessed=4 << 20,
                transcendentals=0,
            ),
        )(tall, taps)

    wide, grad_wide, (pre,) = with_halo(video[0], latent_grad[0], forward)
    row, col = lax.axis_index("row"), lax.axis_index("col")
    flags = jnp.stack(
        [
            frame_counts[0],
            (row > 0).astype(jnp.int32),
            (row < lax.axis_size("row") - 1).astype(jnp.int32),
            (col > 0).astype(jnp.int32),
            (col < lax.axis_size("col") - 1).astype(jnp.int32),
            lax.axis_index("clip"),
        ]
    )
    w_down = kernel_down.reshape(9 * channels, channels)
    kept, sent, own_grad, side_grad, latent = pl.pallas_call(
        main_kernel,
        out_shape=(
            jax.ShapeDtypeStruct((18 * channels, channels), F32),
            jax.ShapeDtypeStruct((18 * channels, channels), BF),
            jax.ShapeDtypeStruct((frames, own, channels), BF),
            jax.ShapeDtypeStruct((ext, 2 * frames, channels), BF),
            jax.ShapeDtypeStruct((outs, channels), BF),
        ),
        in_specs=[pl.BlockSpec(memory_space=pltpu.SMEM)] + [vmem] * 7,
        out_specs=(vmem,) * 5,
        scratch_shapes=[
            pltpu.VMEM((9 * channels, 3 * channels), BF),
            pltpu.VMEM((rows + 4, cols + 8, channels), F32),
            pltpu.VMEM((3, rows + 4, 2 * frames, channels), F32),
            pltpu.VMEM((frames, 3, (rows + 4) * cols, channels), BF),
            pltpu.VMEM((ext, cols, channels), F32),
            pltpu.VMEM((ext, 2 * frames, channels), F32),
            pltpu.VMEM((rows // 2 + 2, 24, channels), F32),
            pltpu.VMEM((frames, ext, cols + 16, channels), F32),
            pltpu.VMEM((ext, 2 * frames, channels), F32),
            pltpu.VMEM((ext, 2 * frames, channels), F32),
            pltpu.VMEM((ext, cols + 16, channels), F32),
            pltpu.VMEM((frames, rows * cols // 4, 9 * channels), BF),
            pltpu.VMEM((frames + 2, channels, rows * cols), BF),
            pltpu.VMEM((9, 2 * channels, channels), F32),
            pltpu.VMEM((9, channels, channels), F32),
        ],
        compiler_params=pltpu.CompilerParams(vmem_limit_bytes=24 << 20),
        cost_estimate=pl.CostEstimate(
            flops=2 * 40 * pixels * channels * channels,
            bytes_accessed=12 << 20,
            transcendentals=pixels * channels,
        ),
    )(
        flags,
        wide,
        grad_wide,
        pre,
        taps,
        grad_matrix(kernel_down),
        w_down,
        latent_grad.reshape(outs, channels),
    )
    video_grad = pl.pallas_call(
        back_kernel,
        out_shape=jax.ShapeDtypeStruct((frames, rows * cols, channels), BF),
        in_specs=[vmem] * 3,
        out_specs=vmem,
        scratch_shapes=[
            pltpu.VMEM((9 * channels, 3 * channels), BF),
            pltpu.VMEM((frames + 2, rows * cols, channels), F32),
            pltpu.VMEM((ext, 2 * frames, channels), F32),
            pltpu.VMEM((ext, cols + 16, channels), F32),
            pltpu.VMEM((GROUP, 3, own, channels), BF),
        ],
        compiler_params=pltpu.CompilerParams(vmem_limit_bytes=12 << 20),
        cost_estimate=pl.CostEstimate(
            flops=2 * 27 * pixels * channels * channels,
            bytes_accessed=4 << 20,
            transcendentals=0,
        ),
    )(own_grad, side_grad, taps)
    main_grad, down_grad, video_grad = reduce_all(kept, sent, video_grad, 27 * channels)
    main_grad = main_grad.reshape(kernel_main.shape)
    down_grad = down_grad.reshape(kernel_down.shape)
    return (latent.reshape(latent_grad.shape), video_grad.reshape(video.shape), main_grad, down_grad)


def solution(mesh):
    tiles = P("clip", None, "row", "col", None)
    return jax.shard_map(
        on_device,
        mesh=mesh,
        in_specs=(tiles, P("clip"), P(), P(), tiles),
        out_specs=(tiles, tiles, P(), P()),
        check_vma=False,
    )
```

```python
import functools

import jax
import jax.numpy as jnp
from jax import lax
from jax.experimental import pallas as pl
from jax.experimental.pallas import tpu as pltpu
from jax.sharding import PartitionSpec as P

BF = jnp.bfloat16
F32 = jnp.float32


def flip(axis, mask):
    return [(i, i ^ mask) for i in range(lax.axis_size(axis))]


def part(x, index, size):
    return lax.dynamic_slice_in_dim(x, index * size, size, axis=0)


def exchange(low_edge, high_edge, axis):
    count = lax.axis_size(axis)
    even = lax.axis_index(axis) % 2 == 0
    inner = [(i, i ^ 1) for i in range(count - count % 2)]
    outer = [(i, ((i + 1) ^ 1) - 1) for i in range(1, count - 1 + count % 2)]
    b = lax.ppermute(jnp.where(even, low_edge, high_edge), axis, outer)
    a = lax.ppermute(jnp.where(even, high_edge, low_edge), axis, inner)
    return jnp.where(even, b, a), jnp.where(even, a, b)


def pack(a, b):
    return jnp.concatenate([a.reshape(-1, a.shape[-1]), b.reshape(-1, b.shape[-1])])


def unpack(buffer, a_shape, b_shape):
    rows = a_shape[0] * a_shape[1] * a_shape[2]
    return buffer[:rows].reshape(a_shape), buffer[rows:].reshape(b_shape)


def edges(video, grad, dim):
    size, gsize = video.shape[dim], grad.shape[dim]
    cut = lax.slice_in_dim
    low = cut(video, 0, 2, axis=dim), cut(grad, 0, 1, axis=dim)
    high = cut(video, size - 2, size, axis=dim), cut(grad, gsize - 1, gsize, axis=dim)
    return low, high


def joined(video, grad, low, high, before, after, dim):
    v_before, g_before = unpack(before, low[0].shape, low[1].shape)
    v_after, g_after = unpack(after, low[0].shape, low[1].shape)
    video = jnp.concatenate([v_before, video, v_after], axis=dim)
    return video, jnp.concatenate([g_before, grad, g_after], axis=dim)


def with_halo(video, grad, forward):
    low, high = edges(video, grad, 1)
    before, after = exchange(pack(*low), pack(*high), "row")
    tall, grad = joined(video, grad, low, high, before, after, 1)
    low, high = edges(tall, grad, 2)
    before, after = exchange(pack(*low), pack(*high), "col")
    (before, after), ready = lax.optimization_barrier(((before, after), forward(tall)))
    return joined(tall, grad, low, high, before, after, 2) + (ready,)


def combine_kernel(index, kept, got, own, *sends):
    share = own.shape[0]
    for mask in range(1 + len(sends)):
        here = pl.ds(pl.multiple_of((index[0] ^ mask) * share, share), share)
        piece = kept[here, :] + got[here, :].astype(F32)
        if mask:
            sends[mask - 1][...] = piece.astype(BF)
        else:
            own[...] = piece


def direct_scatter(kept, got, axis, beside):
    count, mine = lax.axis_size(axis), lax.axis_index(axis)
    shape = (kept.shape[0] // count, kept.shape[1])
    vmem = pl.BlockSpec(memory_space=pltpu.VMEM)
    total, *sends = pl.pallas_call(
        combine_kernel,
        out_shape=(jax.ShapeDtypeStruct(shape, F32),) + (jax.ShapeDtypeStruct(shape, BF),) * (count - 1),
        in_specs=[pl.BlockSpec(memory_space=pltpu.SMEM), vmem, vmem],
        out_specs=(vmem,) * count,
        compiler_params=pltpu.CompilerParams(vmem_limit_bytes=8 << 20),
    )(mine[None], kept, got)
    order = range(count - 1, 0, -1)
    terms = [lax.ppermute(sends[mask - 1], axis, flip(axis, mask)) for mask in order]
    terms, beside = lax.optimization_barrier((terms, beside))
    for term in terms:
        total = total + term.astype(F32)
    return total, beside


def direct_gather(y, axis):
    count, mine = lax.axis_size(axis), lax.axis_index(axis)
    share = y.shape[0]
    whole = jnp.zeros((count * share,) + y.shape[1:], y.dtype)
    whole = lax.dynamic_update_slice_in_dim(whole, y, mine * share, 0)
    for mask in range(count - 1, 0, -1):
        got = lax.ppermute(y, axis, flip(axis, mask))
        whole = lax.dynamic_update_slice_in_dim(whole, got, (mine ^ mask) * share, 0)
    return whole


def half_kernel(which, half, *refs):
    main_grad, down_grad, turned, sems = refs[-4:]
    channels = half.shape[1]
    run = half.shape[0] // 2
    for j in range(2):
        for at in range(j * run, (j + 1) * run, channels):
            turned[at : at + channels, :] = half[at : at + channels, :].astype(F32).T
        source = turned.at[j * run : (j + 1) * run]
        for h in range(2):
            place = 2 * h + j
            target = down_grad if place == 3 else main_grad.at[place * run : (place + 1) * run]

            @pl.when(which[0] == h)
            def _():
                pltpu.make_async_copy(source, target, sems.at[j]).start()

    for j in range(2):
        source = turned.at[j * run : (j + 1) * run]
        pltpu.make_async_copy(source, down_grad, sems.at[j]).wait()


def place_half(which, half, grads, shapes):
    vmem, anywhere = (pl.BlockSpec(memory_space=m) for m in (pltpu.VMEM, pl.ANY))
    return pl.pallas_call(
        half_kernel,
        out_shape=shapes,
        in_specs=[pl.BlockSpec(memory_space=pltpu.SMEM), vmem] + [anywhere] * len(grads),
        out_specs=(anywhere, anywhere),
        input_output_aliases={2 + i: i for i in range(len(grads))},
        scratch_shapes=[pltpu.VMEM(half.shape, F32), pltpu.SemaphoreType.DMA((2,))],
        compiler_params=pltpu.CompilerParams(vmem_limit_bytes=8 << 20),
        cost_estimate=pl.CostEstimate(flops=0, bytes_accessed=4 << 20, transcendentals=0),
    )(which[None], half, *grads)


def reduce_all(kept, sent, beside, main_rows):
    half, core = kept.shape[0], lax.axis_index("clip")
    swap = flip("clip", 1)
    got = lax.ppermute(sent, "clip", swap)
    x, beside = direct_scatter(kept, got, "row", beside)
    count, mine = lax.axis_size("col"), lax.axis_index("col")
    share = x.shape[0] // count
    sums = part(x, mine, share)
    for mask in range(1, count):
        term = lax.ppermute(part(x, mine ^ mask, share).astype(BF), "col", flip("col", mask))
        sums = sums + term.astype(F32)
    y = direct_gather(direct_gather(sums.astype(BF), "col"), "row")
    other = lax.ppermute(y, "clip", swap)
    shapes = (
        jax.ShapeDtypeStruct((main_rows, y.shape[1]), F32),
        jax.ShapeDtypeStruct((2 * half - main_rows, y.shape[1]), F32),
    )
    grads = place_half(core, y, (), shapes)
    other, grads = lax.optimization_barrier((other, grads))
    main_grad, down_grad = place_half(1 - core, other, grads, shapes)
    return main_grad, down_grad, beside


def dot(a, b):
    return lax.dot_general(a, b, (((1,), (0,)), ((), ())), preferred_element_type=F32)


LEFT = 8


GROUP = 4


def side_by_side(kernel_main, w_main):
    channels = kernel_main.shape[1]
    for kt in range(3):
        for tap in range(9):
            rows_at, cols_at = tap * channels, kt * channels
            w_main[rows_at : rows_at + channels, cols_at : cols_at + channels] = kernel_main[9 * kt + tap]


def forward_kernel(tall, kernel_main, pre, w_main, x32, x_taps):
    frames, in_rows, cols, channels = tall.shape
    own = (in_rows - 2) * cols
    side_by_side(kernel_main, w_main)
    x32[...] = jnp.zeros_like(x32)
    for first in range(0, frames, GROUP):
        lines = []
        for g in range(GROUP):
            x32[:, LEFT : LEFT + cols, :] = tall[first + g].astype(F32)
            for kw in range(3):
                shifted = x32[:, pl.ds(LEFT - 1 + kw, cols), :].astype(BF)
                x_taps[g, kw] = shifted.reshape(in_rows * cols, channels)
            taps = [x_taps[g, kw, kh * cols : kh * cols + own] for kh in range(3) for kw in range(3)]
            lines.append(jnp.concatenate(taps, axis=1))
        out = dot(jnp.concatenate(lines, axis=0), w_main[...])
        parts = [out[:, k * channels : (k + 1) * channels] for k in range(3)]
        for g in range(GROUP):
            t, here = first + g, slice(g * own, (g + 1) * own)
            if t == 0:
                pre[0] = parts[0][here] + parts[1][here] + parts[2][here]
                pre[1] = parts[0][here] + parts[1][here]
            else:
                pre[t] += parts[2][here]
                if t + 1 < frames:
                    pre[t + 1] += parts[1][here]
            if t + 2 < frames:
                pre[t + 2] = parts[0][here]


def causal(out, channels):
    first, second, third = (out[..., k * channels : (k + 1) * channels] for k in range(3))
    frames = out.shape[-2]
    start = first[..., 0:1, :]
    back_two = jnp.concatenate([start, start, first[..., : frames - 2, :]], axis=-2)
    back_one = jnp.concatenate([second[..., 0:1, :], second[..., : frames - 1, :]], axis=-2)
    return third + back_one + back_two


def pointwise(v, grad, mask):
    logistic = 1.0 / (1.0 + jnp.exp(-v))
    out = (v * logistic * mask).astype(BF)
    back = (grad * logistic * (1.0 + v * (1.0 - logistic)) * mask).astype(BF)
    return out.astype(F32), back.astype(F32)


def main_kernel(
    flags, wide, grad_wide, pre, kernel_main, w_grad, w_down, latent_grad,
    kept, sent, early_out, late_out, side_out, latent,
    w_main, x32, side32, x_taps, v32, fix, l32, act_grad, side_back, side_act, act,
    act_taps, grad_t, total, down_total,
):
    frames, in_rows, in_cols, channels = wide.shape
    rows, cols = in_rows - 4, in_cols - 4
    ext = rows + 2
    half_rows, half_cols = rows // 2, cols // 2
    own = ext * cols
    grad_t[frames:] = jnp.zeros((2,) + grad_t.shape[1:], BF)
    l32[...] = jnp.zeros_like(l32)
    side_by_side(kernel_main, w_main)
    count = flags[0]
    low_row, high_row = flags[1].astype(F32), flags[2].astype(F32)
    low_col, high_col = flags[3].astype(F32), flags[4].astype(F32)

    def spread(i, carry):
        lines = []
        for g in range(GROUP):
            t = i * GROUP + g
            x32[:, 0:in_cols, :] = wide[t].astype(F32)
            for kw in range(3):
                shifted = x32[:, pl.ds(1 + kw, cols), :].astype(BF)
                x_taps[t, kw] = shifted.reshape(in_rows * cols, channels)
                side32[kw, :, pl.ds(t, 1), :] = x32[:, kw : kw + 1, :]
                side32[kw, :, pl.ds(frames + t, 1), :] = x32[:, cols + 1 + kw : cols + 2 + kw, :]
            l32[:, 0 : half_cols + 2, :] = grad_wide[t].astype(F32)
            near = [l32[:, pl.ds(dq, 16), :].astype(BF) for dq in range(2)]
            shifts = [
                near[dq][dp : dp + half_rows + 1].reshape((half_rows + 1) * 16, channels)
                for dp in (1, 0)
                for dq in (1, 0)
            ]
            lines.append(jnp.concatenate(shifts, axis=1))
        classes = dot(jnp.concatenate(lines, axis=0), w_grad[...])
        for g in range(GROUP):
            t = i * GROUP + g
            for p in range(half_rows + 1):
                at = (g * (half_rows + 1) + p) * 16
                for odd in range(2):
                    line = classes[at : at + half_cols + 1]
                    row = 2 * p + 1 - odd
                    even_part = line[:, 2 * odd * channels : (2 * odd + 1) * channels]
                    odd_part = line[:, (2 * odd + 1) * channels : (2 * odd + 2) * channels]
                    act_grad[t, row, pl.ds(LEFT, half_cols + 1, stride=2), :] = even_part
                    act_grad[t, row, pl.ds(LEFT - 1, half_cols + 1, stride=2), :] = odd_part
            side_back[:, pl.ds(t, 1), :] = act_grad[t, :, LEFT - 1 : LEFT, :]
            side_back[:, pl.ds(frames + t, 1), :] = act_grad[t, :, LEFT + cols : LEFT + cols + 1, :]
        return carry

    lax.fori_loop(0, frames // GROUP, spread, 0)

    side_lhs = jnp.concatenate(
        [
            side32[kw, kh : kh + ext].reshape(ext * 2 * frames, channels).astype(BF)
            for kh in range(3)
            for kw in range(3)
        ],
        axis=1,
    )
    side_pre = dot(side_lhs, w_main[...]).reshape(ext, 2, frames, 3 * channels)
    side_pre = causal(side_pre, channels).reshape(ext, 2 * frames, channels)
    for side in range(2):
        at = side * frames
        lhs = jnp.concatenate(
            [
                side32[1, kh : kh + ext, at : at + frames].reshape(ext * frames, channels).astype(BF)
                for kh in range(3)
            ],
            axis=1,
        )
        weights_here = jnp.concatenate(
            [
                w_main[(3 * kh + 2 * side) * channels : (3 * kh + 2 * side + 1) * channels]
                for kh in range(3)
            ],
            axis=0,
        )
        out = dot(lhs, weights_here).reshape(ext, frames, 3 * channels)
        fix[:, at : at + frames, :] = causal(out, channels)

    def row_mask(width):
        place = lax.broadcasted_iota(jnp.int32, (ext, width, channels), 0)
        return jnp.where(place == 0, low_row, jnp.where(place == ext - 1, high_row, 1.0))

    place = lax.broadcasted_iota(jnp.int32, (ext, 2 * frames, channels), 1)
    side_mask = jnp.where(place < frames, low_col, high_col)
    side_mask = jnp.where(place % frames < count, side_mask, 0.0) * row_mask(2 * frames)
    side_act[...], side_grad = pointwise(side_pre, side_back[...], side_mask)
    side_out[...] = side_grad.astype(BF)

    def frame(own_out, base, t, carry):
        live = jnp.where(t < count, 1.0, 0.0).astype(F32)
        last = frames + t
        v32[...] = pre[t].reshape(ext, cols, channels)
        v32[:, 0:1, :] += fix[:, pl.ds(t, 1), :]
        v32[:, cols - 1 : cols, :] += fix[:, pl.ds(last, 1), :]
        own_act, own_grad = pointwise(
            v32[...], act_grad[t, :, LEFT : LEFT + cols, :], row_mask(cols) * live
        )
        act[:, LEFT : LEFT + cols, :] = own_act
        act[:, LEFT + cols : LEFT + cols + 1, :] = side_act[:, pl.ds(last, 1), :]
        own_out[t - base] = own_grad.reshape(own, channels).astype(BF)
        inner = own_grad.reshape(own, channels)[cols : cols + rows * cols]
        grad_t[t] = inner.T.astype(BF)
        for a in range(3):
            for b in range(3):
                tap = jnp.concatenate(
                    [
                        act[2 * i + a + 1, pl.ds(LEFT + b, half_cols, stride=2), :]
                        for i in range(half_rows)
                    ],
                    axis=0,
                ).astype(BF)
                at = (3 * a + b) * channels
                act_taps[t, :, at : at + channels] = tap
        return carry

    for base, own_out in ((0, early_out), (frames // 2, late_out)):
        lax.fori_loop(base, base + frames // 2, functools.partial(frame, own_out, base), 0)

    flat = act_taps[...].reshape(frames * half_rows * half_cols, 9 * channels)
    latent[...] = dot(flat, w_down[...]).astype(BF)
    down = dot(latent_grad[...].astype(F32).T.astype(BF), flat)
    for tap in range(9):
        down_total[tap] = down[:, tap * channels : (tap + 1) * channels]

    def patches(s):
        taps = [
            x_taps[s, kw, (kh + 1) * cols : (kh + 1 + rows) * cols]
            for kh in range(3)
            for kw in range(3)
        ]
        return jnp.concatenate(taps, axis=1)

    early = dot(grad_t[0:2].reshape(2 * channels, rows * cols), patches(0))
    for tap in range(9):
        block = early[:, tap * channels : (tap + 1) * channels]
        total[tap, 0:channels] = block[:channels]
        total[tap, channels:] = block[:channels] + block[channels:]

    left = [grad_t[t : t + 3].reshape(3 * channels, rows * cols) for t in range(frames)]
    right = [patches(t) for t in range(frames)]
    out = dot(jnp.concatenate(left, axis=1), jnp.concatenate(right, axis=0))

    def emit(low, high):
        for tap in range(9):
            at, after = tap * channels, (9 + tap) * channels
            block = out[:, tap * channels : (tap + 1) * channels]
            first, second, third = (block[k * channels : (k + 1) * channels] for k in (2, 1, 0))
            low[at : at + channels, :] = (first + total[tap, channels:]).astype(low.dtype)
            low[after : after + channels, :] = (second + total[tap, 0:channels]).astype(low.dtype)
            high[at : at + channels, :] = third.astype(high.dtype)
            high[after : after + channels, :] = down_total[tap].astype(high.dtype)

    @pl.when(flags[5] == 0)
    def _():
        emit(kept, sent)

    @pl.when(flags[5] == 1)
    def _():
        emit(sent, kept)


def back_kernel(early_grad, late_grad, side_grad, kernel_main, video_grad, w_back, total, side32, g32, grad_taps):
    half, own, channels = early_grad.shape
    frames = 2 * half
    inner = video_grad.shape[1]
    cols = (own - inner) // 2
    ext = own // cols
    side32[...] = side_grad[...].astype(F32)
    total[0:2] = jnp.zeros((2,) + total.shape[1:], F32)
    for kt in range(3):
        for tap in range(9):
            rows_at, cols_at = tap * channels, kt * channels
            block = kernel_main[9 * kt + 8 - tap].astype(F32).T.astype(BF)
            w_back[rows_at : rows_at + channels, cols_at : cols_at + channels] = block

    def group(own_grad, i, carry):
        lines = []
        for g in range(GROUP):
            t = i * GROUP + g
            g32[:, LEFT : LEFT + cols, :] = own_grad[t % half].astype(F32).reshape(ext, cols, channels)
            g32[:, LEFT - 1 : LEFT, :] = side32[:, pl.ds(t, 1), :]
            g32[:, LEFT + cols : LEFT + cols + 1, :] = side32[:, pl.ds(frames + t, 1), :]
            for kw in range(3):
                shifted = g32[:, pl.ds(LEFT - 1 + kw, cols), :].astype(BF)
                grad_taps[g, kw] = shifted.reshape(own, channels)
            taps = [
                grad_taps[g, kw, kh * cols : kh * cols + inner]
                for kh in range(3)
                for kw in range(3)
            ]
            lines.append(jnp.concatenate(taps, axis=1))
        out = dot(jnp.concatenate(lines, axis=0), w_back[...])
        parts = [out[:, k * channels : (k + 1) * channels] for k in range(3)]
        for g in range(GROUP):
            t, here = i * GROUP + g, slice(g * inner, (g + 1) * inner)
            total[t + 2] = parts[2][here]
            total[t + 1] += parts[1][here]
            total[t] += parts[0][here]
        return carry

    for base, own_grad in ((0, early_grad), (half, late_grad)):
        first, last = base // GROUP, (base + half) // GROUP
        lax.fori_loop(first, last, functools.partial(group, own_grad), 0)
    video_grad[0] = (total[0] + total[1] + total[2]).astype(BF)

    def store(t, carry):
        video_grad[t] = total[t + 2].astype(BF)
        return carry

    lax.fori_loop(1, frames, store, 0)


def grad_matrix(kernel_down):
    k = jnp.swapaxes(kernel_down, 2, 3)
    zero = jnp.zeros_like(k[0, 0])
    return jnp.concatenate(
        [
            jnp.concatenate([k[0, 0], zero, zero, zero], axis=1),
            jnp.concatenate([k[0, 2], k[0, 1], zero, zero], axis=1),
            jnp.concatenate([k[2, 0], zero, k[1, 0], zero], axis=1),
            jnp.concatenate([k[2, 2], k[2, 1], k[1, 2], k[1, 1]], axis=1),
        ]
    )


def on_device(video, frame_counts, kernel_main, kernel_down, latent_grad):
    _, frames, rows, cols, channels = video.shape
    ext = rows + 2
    own, outs = ext * cols, frames * rows * cols // 4
    pixels = frames * rows * cols
    vmem = pl.BlockSpec(memory_space=pltpu.VMEM)
    taps = kernel_main.reshape(27, channels, channels)

    def forward(tall):
        return pl.pallas_call(
            forward_kernel,
            out_shape=(
                jax.ShapeDtypeStruct((frames, own, channels), F32),
            ),
            in_specs=[vmem] * 2,
            out_specs=(vmem,),
            scratch_shapes=[
                pltpu.VMEM((9 * channels, 3 * channels), BF),
                pltpu.VMEM((rows + 4, cols + 16, channels), F32),
                pltpu.VMEM((GROUP, 3, (rows + 4) * cols, channels), BF),
            ],
            compiler_params=pltpu.CompilerParams(vmem_limit_bytes=16 << 20),
            cost_estimate=pl.CostEstimate(
                flops=2 * 27 * frames * own * channels * channels,
                bytes_accessed=4 << 20,
                transcendentals=0,
            ),
        )(tall, taps)

    wide, grad_wide, (pre,) = with_halo(video[0], latent_grad[0], forward)
    row, col = lax.axis_index("row"), lax.axis_index("col")
    flags = jnp.stack(
        [
            frame_counts[0],
            (row > 0).astype(jnp.int32),
            (row < lax.axis_size("row") - 1).astype(jnp.int32),
            (col > 0).astype(jnp.int32),
            (col < lax.axis_size("col") - 1).astype(jnp.int32),
            lax.axis_index("clip"),
        ]
    )
    w_down = kernel_down.reshape(9 * channels, channels)
    kept, sent, early_grad, late_grad, side_grad, latent = pl.pallas_call(
        main_kernel,
        out_shape=(
            jax.ShapeDtypeStruct((18 * channels, channels), F32),
            jax.ShapeDtypeStruct((18 * channels, channels), BF),
            jax.ShapeDtypeStruct((frames // 2, own, channels), BF),
            jax.ShapeDtypeStruct((frames // 2, own, channels), BF),
            jax.ShapeDtypeStruct((ext, 2 * frames, channels), BF),
            jax.ShapeDtypeStruct((outs, channels), BF),
        ),
        in_specs=[pl.BlockSpec(memory_space=pltpu.SMEM)] + [vmem] * 7,
        out_specs=(vmem,) * 6,
        scratch_shapes=[
            pltpu.VMEM((9 * channels, 3 * channels), BF),
            pltpu.VMEM((rows + 4, cols + 8, channels), F32),
            pltpu.VMEM((3, rows + 4, 2 * frames, channels), F32),
            pltpu.VMEM((frames, 3, (rows + 4) * cols, channels), BF),
            pltpu.VMEM((ext, cols, channels), F32),
            pltpu.VMEM((ext, 2 * frames, channels), F32),
            pltpu.VMEM((rows // 2 + 2, 24, channels), F32),
            pltpu.VMEM((frames, ext, cols + 16, channels), F32),
            pltpu.VMEM((ext, 2 * frames, channels), F32),
            pltpu.VMEM((ext, 2 * frames, channels), F32),
            pltpu.VMEM((ext, cols + 16, channels), F32),
            pltpu.VMEM((frames, rows * cols // 4, 9 * channels), BF),
            pltpu.VMEM((frames + 2, channels, rows * cols), BF),
            pltpu.VMEM((9, 2 * channels, channels), F32),
            pltpu.VMEM((9, channels, channels), F32),
        ],
        compiler_params=pltpu.CompilerParams(vmem_limit_bytes=24 << 20),
        cost_estimate=pl.CostEstimate(
            flops=2 * 40 * pixels * channels * channels,
            bytes_accessed=12 << 20,
            transcendentals=pixels * channels,
        ),
    )(
        flags,
        wide,
        grad_wide,
        pre,
        taps,
        grad_matrix(kernel_down),
        w_down,
        latent_grad.reshape(outs, channels),
    )
    video_grad = pl.pallas_call(
        back_kernel,
        out_shape=jax.ShapeDtypeStruct((frames, rows * cols, channels), BF),
        in_specs=[vmem] * 4,
        out_specs=vmem,
        scratch_shapes=[
            pltpu.VMEM((9 * channels, 3 * channels), BF),
            pltpu.VMEM((frames + 2, rows * cols, channels), F32),
            pltpu.VMEM((ext, 2 * frames, channels), F32),
            pltpu.VMEM((ext, cols + 16, channels), F32),
            pltpu.VMEM((GROUP, 3, own, channels), BF),
        ],
        compiler_params=pltpu.CompilerParams(vmem_limit_bytes=12 << 20),
        cost_estimate=pl.CostEstimate(
            flops=2 * 27 * pixels * channels * channels,
            bytes_accessed=4 << 20,
            transcendentals=0,
        ),
    )(early_grad, late_grad, side_grad, taps)
    main_grad, down_grad, video_grad = reduce_all(kept, sent, video_grad, 27 * channels)
    main_grad = main_grad.reshape(kernel_main.shape)
    down_grad = down_grad.reshape(kernel_down.shape)
    return (latent.reshape(latent_grad.shape), video_grad.reshape(video.shape), main_grad, down_grad)


def solution(mesh):
    tiles = P("clip", None, "row", "col", None)
    return jax.shard_map(
        on_device,
        mesh=mesh,
        in_specs=(tiles, P("clip"), P(), P(), tiles),
        out_specs=(tiles, tiles, P(), P()),
        check_vma=False,
    )
```
